32 devices in a mesh: dp: 4 (over y, core), tensor: 8 (over z, x).
Axes of the slice: x: 2, y: 2, z: 4, core: 2. Of those that a mesh axis runs over, the one named last changes fastest.
Arguments:
- tokens: bfloat16 [8192, 2048], P(('dp', 'tensor')), may hold values from -6 to 6
- segment_ids: int32 [4, 2048], P('dp'), may hold values from 0 to 3, never falling along the last dimension, each value on 1 to 1024 neighbouring positions
- first_gain: bfloat16 [2048], replicated, may hold values from 0.5 to 1.5
- first_shift: bfloat16 [2048], replicated, may hold values from -3 to 3
- second_gain: bfloat16 [2048], replicated, may hold values from 0.5 to 1.5
- second_shift: bfloat16 [2048], replicated, may hold values from -3 to 3
- qkv_weight: bfloat16 [2048, 8, 768], P('dp', 'tensor'), may hold values from -0.125 to 0.125
- qkv_bias: bfloat16 [8, 768], P('tensor'), may hold values from -3 to 3
- out_weight: bfloat16 [2048, 2048], P('tensor', 'dp'), may hold values from -1 to 1
- out_bias: bfloat16 [2048], replicated, may hold values from -3 to 3
- up_projection_weight: bfloat16 [2048, 8192], P('dp', 'tensor'), may hold values from -0.125 to 0.125
- up_bias: bfloat16 [8192], P('tensor'), may hold values from -3 to 3
- down_weight: bfloat16 [8192, 2048], P('tensor', 'dp'), may hold values from -0.0625 to 0.0625
- down_bias: bfloat16 [2048], replicated, may hold values from -3 to 3
- cotangent: bfloat16 [8192, 2048], P(('dp', 'tensor')), may hold values from -6 to 6
Outputs:
- output: bfloat16 [8192, 2048], P(('dp', 'tensor'))
- layer_input_gradient: float32 [8192, 2048], P(('dp', 'tensor'))
- first_gain_grad: float32 [2048], replicated
- first_shift_grad: float32 [2048], replicated
- second_gain_grad: float32 [2048], replicated
- second_shift_grad: float32 [2048], replicated
- qkv_weight_grad: float32 [2048, 8, 768], P('dp', 'tensor')
- qkv_bias_grad: float32 [8, 768], P('tensor')
- out_weight_grad: float32 [2048, 2048], P('tensor', 'dp')
- out_bias_grad: float32 [2048], replicated
- up_weight_grad: float32 [2048, 8192], P('dp', 'tensor')
- up_bias_grad: float32 [8192], P('tensor')
- down_weight_grad: float32 [8192, 2048], P('tensor', 'dp')
- down_bias_grad: float32 [2048], replicated
The draws below stay inside these ranges and needn't reach their ends.
Inputs may be any that keep to these rules, and one draw needn't show every extreme that they name: `segment_ids`: within each group the segment numbers never fall; each sequence has 1 to 1024 tokens and one of them exactly 1024; every number up to the largest occurs.
All inputs are finite; a program needn't handle non-finite values.
Results may differ from the reference program's by a relative error of at most 0.014.
Values may be sent and summed in bfloat16 or wider, within the bound.
No kernel may reach another device: no remote copies, remote signals or barrier semaphores. Data moves between devices by JAX's collectives and lax.ppermute only.
A program may use at most 192 MiB of HBM per device.

```python
import math
import jax
import jax.numpy as jnp
import numpy as np
from jax import lax

MODEL_WIDTH = 2048
H = 8
HD = 256
ROT = 64
FF = 8192
TOK_GROUP = 2048
LONGEST = 1024
SEGS = 4
TOKENS = 8192
N_DP = 4
N_TENSOR = 8


def block_levels(key, extent, shards, smallest, top_value):
    loudness = 1.0
    for dim, shards_of in shards:
        steps = jax.random.uniform(jax.random.fold_in(jax.random.fold_in(key, 6), dim), (shards_of,), jnp.float32, smallest / len(shards), top_value / len(shards))
        loudness = loudness * jnp.repeat(jnp.exp(steps), extent[dim] // shards_of).reshape((-1,) + (1,) * (len(extent) - 1 - dim))
    return loudness


def length_profile(count, total, bound, lean):
    portions = [(1 << 20) // math.isqrt(grade ** lean) + 1 for grade in range(2, count + 1)]
    surplus, counts = total - bound - (count - 1), [1] * (count - 1)
    while surplus > 0:
        candidates = [i for i in range(count - 1) if counts[i] < bound]
        whole, left = sum([portions[i] for i in candidates]), surplus
        for i in candidates:
            addition = min(bound - counts[i], max(1, left * portions[i] // whole), surplus)
            counts[i] = counts[i] + addition
            surplus = surplus - addition
    return np.array([bound] + counts)


def ragged_sizes(own_key, count, total, bound, skew):
    if count == 2:
        one = jax.random.randint(own_key, (), max(1, total - bound), min(bound, total - 1) + 1)
        return jnp.stack([one, total - one])
    tallies = jnp.asarray(length_profile(count, total, bound, skew), jnp.int32)
    pairs = (count - 1) // 2
    source_of, receiver = tallies[1:1 + 2 * pairs:2], tallies[2:2 + 2 * pairs:2]
    slack = jnp.minimum(source_of - 1, bound - receiver)
    passed = jax.random.randint(jax.random.fold_in(own_key, 1), (pairs,), 0, 1 << 20) % (slack + 1)
    tallies = tallies.at[1:1 + 2 * pairs:2].set(source_of - passed).at[2:2 + 2 * pairs:2].set(receiver + passed)
    return tallies[jax.random.permutation(jax.random.fold_in(own_key, 2), count)]


def normal_values(key, shape, scale, reach, split=(), held_as=jnp.bfloat16):
    gain = block_levels(key, shape, split, -0.22, 0.18) if split else 1.0
    drawn = jax.random.normal(key, shape, jnp.float32) * scale * gain
    return jnp.minimum(jnp.maximum(drawn, -reach), reach).astype(held_as)


def setup_inputs(seed: int = 0) -> dict:
    streams_of = jax.random.split(jax.random.key(seed), 16)
    tokens = normal_values(streams_of[0], (TOKENS, MODEL_WIDTH), 1.0, 6.0, ((0, 32),))
    segment_ids = jax.vmap(lambda own: jnp.searchsorted(jnp.cumsum(ragged_sizes(own, SEGS, TOK_GROUP, LONGEST, 2)), jnp.arange(TOK_GROUP), side="right"))(jax.random.split(streams_of[1], N_DP)).reshape((N_DP, TOK_GROUP)).astype(jnp.int32)
    first_gain = jnp.clip(1.0 + 0.1 * jax.random.normal(streams_of[2], (MODEL_WIDTH,), jnp.float32), 0.5, 1.5).astype(jnp.bfloat16)
    first_shift = normal_values(streams_of[3], (MODEL_WIDTH,), 0.5, 3.0)
    second_gain = jnp.clip(1.0 + 0.1 * jax.random.normal(streams_of[4], (MODEL_WIDTH,), jnp.float32), 0.5, 1.5).astype(jnp.bfloat16)
    second_shift = normal_values(streams_of[5], (MODEL_WIDTH,), 0.5, 3.0)
    qkv_weight = normal_values(streams_of[6], (MODEL_WIDTH, H, 3 * HD), MODEL_WIDTH ** -0.5, 0.125, ((0, 4), (1, 8)))
    qkv_bias = normal_values(streams_of[7], (H, 3 * HD), 0.5, 3.0, ((0, 8),))
    out_weight = normal_values(streams_of[8], (H * HD, MODEL_WIDTH), (MODEL_WIDTH // 64) ** -0.5, 1.0, ((0, 8), (1, 4)))
    out_bias = normal_values(streams_of[9], (MODEL_WIDTH,), 0.5, 3.0)
    up_projection_weight = normal_values(streams_of[10], (MODEL_WIDTH, FF), MODEL_WIDTH ** -0.5, 0.125, ((0, 4), (1, 8)))
    up_bias = normal_values(streams_of[11], (FF,), 0.5, 3.0, ((0, 8),))
    down_weight = normal_values(streams_of[12], (FF, MODEL_WIDTH), FF ** -0.5, 0.0625, ((0, 8), (1, 4)))
    down_bias = normal_values(streams_of[13], (MODEL_WIDTH,), 0.5, 3.0)
    cotangent = normal_values(streams_of[14], (TOKENS, MODEL_WIDTH), 1.0, 6.0, ((0, 32),))
    return dict(tokens=tokens, segment_ids=segment_ids, first_gain=first_gain, first_shift=first_shift, second_gain=second_gain, second_shift=second_shift, qkv_weight=qkv_weight, qkv_bias=qkv_bias, out_weight=out_weight, out_bias=out_bias, up_projection_weight=up_projection_weight, up_bias=up_bias, down_weight=down_weight, down_bias=down_bias, cotangent=cotangent)


NORM_EPS = 1e-05
MASK_FILL = -1e+30
TOP_PRECISION = lax.Precision.HIGHEST

@jax.custom_vjp
def low(v):
    return lax.optimization_barrier(v.astype(jnp.bfloat16)).astype(jnp.float32)

@jax.custom_vjp
def low_back(v):
    return v

def low_keep(v):
    return (low(v), None)

def low_pass(kept, grad):
    return (grad,)

def back_keep(v):
    return (v, None)

def back_low(kept, grad):
    return (low(grad),)
low.defvjp(low_keep, low_pass)
low_back.defvjp(back_keep, back_low)

def positions_of(segment):
    row_count = segment.shape[0]
    position_index = jnp.arange(row_count, dtype=jnp.int32)
    starts = jnp.concatenate([jnp.ones((1,), dtype=jnp.bool_), segment[1:] != segment[:-1]])
    first_index = lax.cummax(jnp.where(starts, position_index, jnp.zeros_like(position_index)), axis=0)
    return position_index - first_index

def rotation_tables(position):
    half_dims = ROT // 2
    inv_freq = 10000.0 ** (-2.0 * jnp.arange(half_dims, dtype=jnp.float32) / ROT)
    angles = position.astype(jnp.float32)[:, None] * inv_freq[None, :]
    return (jnp.cos(angles), jnp.sin(angles))

def rotate(values, cosine_table, sine_table):
    half_dims = ROT // 2
    leading = values[..., :half_dims]
    trailing = values[..., half_dims:ROT]
    return jnp.concatenate([leading * cosine_table - trailing * sine_table, trailing * cosine_table + leading * sine_table, values[..., ROT:]], axis=-1)

def normalize(values):
    mean_val = lax.optimization_barrier(jnp.mean(values, axis=-1, keepdims=True))
    centred = values - mean_val
    spread = lax.optimization_barrier(jnp.mean(centred * centred, axis=-1, keepdims=True))
    return centred * lax.rsqrt(spread + NORM_EPS)

def group_forward(x_values, segment, first_gain, first_shift, second_gain, second_shift, qkv_weight, qkv_bias, out_weight, out_bias, up_projection_weight, up_bias, down_weight, down_bias):
    row_count = x_values.shape[0]
    heads_here = H // N_TENSOR
    local_hidden_units = FF // N_TENSOR
    position = positions_of(segment)
    cosine_table, sine_table = rotation_tables(position)
    normed_low = low(normalize(x_values))
    normed_copies = low_back(jnp.broadcast_to(normed_low, (N_TENSOR, row_count, MODEL_WIDTH)))
    first_copies = low(normed_copies * first_gain + first_shift)
    second_replicas = low(normed_copies * second_gain + second_shift)
    proj = jnp.einsum('rgd,drhk->rhgk', first_copies, qkv_weight.reshape(MODEL_WIDTH, N_TENSOR, heads_here, 3 * HD), precision=TOP_PRECISION)
    proj = low_back(proj + qkv_bias.reshape(N_TENSOR, heads_here, 1, 3 * HD))
    query = low(rotate(proj[..., :HD], cosine_table, sine_table))
    key_all = low(rotate(proj[..., HD:2 * HD], cosine_table, sine_table))
    value = low(proj[..., 2 * HD:])
    raw = low_back(jnp.einsum('rhqd,rhkd->rhqk', query, key_all, precision=TOP_PRECISION) * (1.0 / math.sqrt(HD)))
    position_index = jnp.arange(row_count, dtype=jnp.int32)
    allowed = (segment[:, None] == segment[None, :]) & (position_index[:, None] >= position_index[None, :])
    scores = jnp.where(allowed, raw, MASK_FILL)
    row_top = lax.optimization_barrier(jnp.max(scores, axis=-1, keepdims=True))
    exp_scores = jnp.exp(scores - row_top)
    probs = exp_scores / lax.optimization_barrier(jnp.sum(exp_scores, axis=-1, keepdims=True))
    attn = jnp.einsum('rhqk,rhkd->rhqd', low(probs), value, precision=TOP_PRECISION)
    attn = low(low_back(attn))
    attn_part = jnp.einsum('rhgd,rhde->rge', attn, out_weight.reshape(N_TENSOR, heads_here, HD, MODEL_WIDTH), precision=TOP_PRECISION)
    up_preactivation = jnp.einsum('yxz,zyo->yxo', second_replicas, up_projection_weight.reshape(MODEL_WIDTH, N_TENSOR, local_hidden_units), precision=TOP_PRECISION)
    up_preactivation = low_back(up_preactivation + up_bias.reshape(N_TENSOR, 1, local_hidden_units))
    act = low(jax.nn.gelu(up_preactivation, approximate=False))
    mlp_part = jnp.einsum('rgf,rfe->rge', act, down_weight.reshape(N_TENSOR, local_hidden_units, MODEL_WIDTH), precision=TOP_PRECISION)
    branch_total = lax.optimization_barrier(jnp.sum(low(attn_part + mlp_part), axis=0))
    return x_values + out_bias + down_bias + branch_total

def reference(tokens, segment_ids, first_gain, first_shift, second_gain, second_shift, qkv_weight, qkv_bias, out_weight, out_bias, up_projection_weight, up_bias, down_weight, down_bias, cotangent):
    params = tuple((member.astype(jnp.float32) for member in (first_gain, first_shift, second_gain, second_shift, qkv_weight, qkv_bias, out_weight, out_bias, up_projection_weight, up_bias, down_weight, down_bias)))
    token_groups = tokens.reshape(N_DP, TOK_GROUP, MODEL_WIDTH)
    cot_groups = cotangent.reshape(N_DP, TOK_GROUP, MODEL_WIDTH)

    def one_group(running, member):
        x_group, segment, cot_group = member

        def forward(x_in, *weights):
            return group_forward(x_in, segment, *weights)
        result, pull = jax.vjp(forward, x_group.astype(jnp.float32), *params)
        grads = pull(cot_group.astype(jnp.float32))
        updated = tuple((accum + extra for accum, extra in zip(running, grads[1:])))
        return (updated, (result.astype(jnp.bfloat16), grads[0]))
    init_sums = tuple((jnp.zeros(member.shape, jnp.float32) for member in params))
    sums_all, (outs_all, input_grads) = lax.scan(one_group, init_sums, (token_groups, segment_ids, cot_groups))
    return (outs_all.reshape(TOKENS, MODEL_WIDTH), input_grads.reshape(TOKENS, MODEL_WIDTH), sums_all[0], sums_all[1], sums_all[2], sums_all[3], sums_all[4], sums_all[5], sums_all[6], sums_all[7], sums_all[8], sums_all[9], sums_all[10], sums_all[11])
```

```python
import math

import jax
import jax.numpy as jnp
from jax import lax
from jax.sharding import PartitionSpec as P

HD = 256
ROT = 64

NORM_EPS = 1e-05
MASK_FILL = -1e30
F32 = jnp.float32
BF16 = jnp.bfloat16


def normalize(values):
    mean_val = jnp.mean(values, axis=-1, keepdims=True)
    centred = values - mean_val
    spread = jnp.mean(centred * centred, axis=-1, keepdims=True)
    inv_std = lax.rsqrt(spread + NORM_EPS)
    return (centred * inv_std, inv_std)


def positions_of(segment):
    row_count = segment.shape[0]
    position_index = jnp.arange(row_count, dtype=jnp.int32)
    starts = jnp.concatenate([jnp.ones((1,), dtype=jnp.bool_), segment[1:] != segment[:-1]])
    first_index = lax.cummax(
        jnp.where(starts, position_index, jnp.zeros_like(position_index)), axis=0
    )
    return position_index - first_index


def rotation_tables(position):
    half_dims = ROT // 2
    inv_freq = 10000.0 ** (-2.0 * jnp.arange(half_dims, dtype=jnp.float32) / ROT)
    angles = position.astype(jnp.float32)[:, None] * inv_freq[None, :]
    return (jnp.cos(angles), jnp.sin(angles))


def rotate(values, cosine_table, sine_table, direction):
    half_dims = ROT // 2
    leading = values[:, :half_dims]
    trailing = values[:, half_dims:ROT]
    return jnp.concatenate(
        [
            leading * cosine_table - direction * trailing * sine_table,
            trailing * cosine_table + direction * leading * sine_table,
            values[:, ROT:],
        ],
        axis=1,
    )


def after(value, *others):
    return lax.optimization_barrier((value,) + others)[0]


class Ring:
    def __init__(self, axis):
        self.axis = axis
        size = lax.axis_size(axis)
        order = list(range(0, size, 2)) + list(range(size - 1, 0, -2))
        self.size = size
        self.order = jnp.array(order, jnp.int32)
        place = [order.index(i) for i in range(size)]
        self.place = jnp.array(place, jnp.int32)[lax.axis_index(axis)]
        self.up = [(order[i], order[(i + 1) % size]) for i in range(size)]
        self.down = [(order[i], order[(i - 1) % size]) for i in range(size)]

    def index(self, offset):
        return self.order[(self.place + offset) % self.size]

    def send_up(self, value):
        return lax.ppermute(value, self.axis, self.up)

    def send_down(self, value):
        return lax.ppermute(value, self.axis, self.down)

    def gather(self, block):
        half = block.shape[0] // 2
        got = [(0, block)]
        up = down = block
        for step in range(1, self.size // 2):
            up, down = self.send_up(up), self.send_down(down)
            got += [(-step, up), (step, down)]
        far = jnp.concatenate([self.send_up(up[:half]), self.send_down(down[half:])], axis=0)
        got.append((self.size // 2, far))
        return got, (up, down)

    def place_rows(self, got):
        rows, cols = got[0][1].shape
        whole = jnp.zeros((rows * self.size, cols), got[0][1].dtype)
        for offset, block in got:
            whole = lax.dynamic_update_slice(whole, block, (self.index(offset) * rows, 0))
        return whole

    def scatter_sum(self, part, rows, cols, pieces):
        half, width = rows // 2, cols // pieces
        result = []
        far = self.size // 2
        for piece in range(pieces):
            window = (piece * width, width)
            arrived = []
            for send, sign, start in ((self.send_up, 1, 0), (self.send_down, -1, half)):
                first = self.index(sign * far) * rows + start
                moving = send(part(first, half, window).astype(BF16)).astype(F32)
                for step in range(far - 1, 0, -1):
                    own = part(self.index(sign * step) * rows, rows, window)
                    if step == far - 1:
                        pad = ((0, rows - half), (0, 0)) if start == 0 else ((half, 0), (0, 0))
                        moving = jnp.pad(moving, pad)
                    moving = send((own + moving).astype(BF16)).astype(F32)
                arrived.append(moving)
            own = part(self.index(0) * rows, rows, window)
            result.append(own + arrived[0] + arrived[1])
        return jnp.concatenate(result, axis=1)


def doubling_sum(value, axis):
    size = lax.axis_size(axis)
    step = 1
    while step < size:
        value = value + lax.ppermute(value, axis, [(i, i ^ step) for i in range(size)])
        step *= 2
    return value


def doubling_gather(value, axis):
    size = lax.axis_size(axis)
    me = lax.axis_index(axis)
    step = 1
    while step < size:
        other = lax.ppermute(value, axis, [(i, i ^ step) for i in range(size)])
        upper = (me & step) != 0
        value = jnp.where(
            upper,
            jnp.concatenate([other, value], axis=1),
            jnp.concatenate([value, other], axis=1),
        )
        step *= 2
    return value


def body(
    tokens,
    segment_ids,
    first_gain,
    first_shift,
    second_gain,
    second_shift,
    qkv_weight,
    qkv_bias,
    out_weight,
    out_bias,
    up_projection_weight,
    up_bias,
    down_weight,
    down_bias,
    cotangent,
):
    width = tokens.shape[1]
    rows = tokens.shape[0]
    qkv_cols = 3 * HD
    segment = segment_ids[0]
    group_rows = segment.shape[0]
    block_rows = min(512, group_rows)
    block_count = group_rows // block_rows
    ring = Ring("tensor")
    shard_rows = qkv_weight.shape[0]
    dp_start = lax.axis_index("dp") * shard_rows

    w_qkv = qkv_weight.reshape(shard_rows, qkv_cols).astype(F32)
    w_up = up_projection_weight.astype(F32)

    def shard(vector):
        return lax.dynamic_slice(vector, (dp_start,), (shard_rows,)).astype(F32)

    gain1, gain2 = shard(first_gain), shard(second_gain)
    shift1, shift2 = shard(first_shift), shard(second_shift)
    scaled = jnp.concatenate(
        [w_qkv * gain1[:, None], w_up * gain2[:, None]], axis=1
    ).astype(BF16)
    w_in = lax.all_gather(scaled, "dp", axis=0, tiled=True)
    shift_part = jnp.concatenate(
        [jnp.sum(w_qkv * shift1[:, None], axis=0), jnp.sum(w_up * shift2[:, None], axis=0)]
    )
    in_bias = doubling_sum(shift_part[None], "dp")[0] + jnp.concatenate(
        [qkv_bias.reshape(-1), up_bias]
    ).astype(F32)
    w_out = lax.all_gather(
        jnp.concatenate([out_weight, down_weight], axis=0), "dp", axis=1, tiled=True
    )

    x_values = tokens.astype(F32)
    normed, inv_std = normalize(x_values)
    token_blocks, token_last = ring.gather(normed.astype(BF16))
    normed_all = ring.place_rows(token_blocks)
    cot_blocks, cot_last = ring.gather(after(cotangent, token_last[0], token_last[1]))
    cot_all = ring.place_rows(cot_blocks)

    position = positions_of(segment)
    cosine_table, sine_table = rotation_tables(position)
    position_index = jnp.arange(group_rows, dtype=jnp.int32)
    score_scale = 1.0 / math.sqrt(HD)

    proj = (
        jnp.dot(normed_all, w_in[:, :qkv_cols], preferred_element_type=F32)
        + in_bias[None, :qkv_cols]
    )
    query = rotate(proj[:, :HD], cosine_table, sine_table, 1.0).astype(BF16)
    key = rotate(proj[:, HD : 2 * HD], cosine_table, sine_table, 1.0).astype(BF16)
    value = proj[:, 2 * HD :].astype(BF16)
    up = (
        jnp.dot(normed_all, w_in[:, qkv_cols:], preferred_element_type=F32)
        + in_bias[None, qkv_cols:]
    )
    cdf = 0.5 * (1.0 + lax.erf(up * (1.0 / math.sqrt(2.0))))
    act = (up * cdf).astype(BF16)
    slope = (cdf + up * (jnp.exp(-0.5 * up * up) * (1.0 / math.sqrt(2.0 * math.pi)))).astype(BF16)

    def block_scores(row_start, key_count):
        raw = (
            jnp.einsum(
                "qd,kd->qk",
                query[row_start:key_count],
                key[:key_count],
                preferred_element_type=F32,
            )
            * score_scale
        )
        seg_query = segment[row_start:key_count]
        allowed = (seg_query[:, None] == segment[None, :key_count]) & (
            position_index[row_start:key_count, None] >= position_index[None, :key_count]
        )
        return jnp.where(allowed, raw, MASK_FILL)

    rows_out = []
    lse_rows = []
    for block_index in range(block_count):
        row_start = block_index * block_rows
        key_count = row_start + block_rows
        scores = block_scores(row_start, key_count)
        row_top = jnp.max(scores, axis=1, keepdims=True)
        exp_scores = jnp.exp(scores - row_top)
        row_total = jnp.sum(exp_scores, axis=1, keepdims=True)
        probs_low = (exp_scores / row_total).astype(BF16)
        rows_out.append(
            jnp.dot(probs_low, value[:key_count], preferred_element_type=F32).astype(BF16)
        )
        lse_rows.append(row_top + jnp.log(row_total))
    attn = jnp.concatenate(rows_out, axis=0)
    lse = jnp.concatenate(lse_rows, axis=0)
    mixed = jnp.concatenate([attn, act], axis=1)

    mixed_out = after(mixed, cot_last[0], cot_last[1])

    def out_part(first, count, window):
        block = lax.dynamic_slice(mixed_out, (first, 0), (count, mixed.shape[1]))
        return jnp.dot(
            block, w_out[:, window[0] : window[0] + window[1]], preferred_element_type=F32
        )

    summed = ring.scatter_sum(out_part, rows, width, 2)
    output = (x_values + out_bias.astype(F32) + down_bias.astype(F32) + summed).astype(BF16)

    back_mixed = jnp.einsum("gd,fd->gf", cot_all, w_out, preferred_element_type=F32)
    d_attn = back_mixed[:, :HD].astype(BF16)
    d_up = (back_mixed[:, HD:] * slope.astype(F32)).astype(BF16)
    query_grads = []
    key_grad = jnp.zeros((group_rows, HD), F32)
    value_grad = jnp.zeros((group_rows, HD), F32)
    for block_index in range(block_count):
        row_start = block_index * block_rows
        key_count = row_start + block_rows
        scores = block_scores(row_start, key_count)
        probs = jnp.exp(scores - lse[row_start:key_count])
        grad_block = d_attn[row_start:key_count]
        d_probs = jnp.einsum(
            "qd,kd->qk", grad_block, value[:key_count], preferred_element_type=F32
        )
        d_scores = (probs * (d_probs - jnp.sum(probs * d_probs, axis=1, keepdims=True))).astype(
            BF16
        )
        query_grads.append(
            jnp.dot(d_scores, key[:key_count], preferred_element_type=F32) * score_scale
        )
        key_grad = key_grad.at[:key_count].add(
            jnp.einsum(
                "qk,qd->kd", d_scores, query[row_start:key_count], preferred_element_type=F32
            )
            * score_scale
        )
        value_grad = value_grad.at[:key_count].add(
            jnp.einsum("qk,qd->kd", probs.astype(BF16), grad_block, preferred_element_type=F32)
        )
    query_grad = rotate(jnp.concatenate(query_grads, axis=0), cosine_table, sine_table, -1.0)
    key_grad = rotate(key_grad, cosine_table, sine_table, -1.0)
    d_proj = jnp.concatenate([query_grad, key_grad, value_grad], axis=1).astype(BF16)
    d_in = jnp.concatenate([d_proj, d_up], axis=1)

    def grad_piece(first, count, window):
        block = lax.dynamic_slice(d_in, (first, 0), (count, d_in.shape[1]))
        return jnp.einsum(
            "gf,df->gd",
            block,
            w_in[window[0] : window[0] + window[1]],
            preferred_element_type=F32,
        )

    grad_normed = ring.scatter_sum(grad_piece, rows, width, 2)
    cot_values = cotangent.astype(F32)
    layer_input_gradient = cot_values + inv_std * (
        grad_normed
        - jnp.mean(grad_normed, axis=1, keepdims=True)
        - normed * jnp.mean(grad_normed * normed, axis=1, keepdims=True)
    )

    out_grad = lax.psum_scatter(
        jnp.einsum("gd,gf->df", cot_all, mixed, preferred_element_type=F32).astype(BF16),
        "dp",
        scatter_dimension=0,
        tiled=True,
    )
    out_grad = out_grad.astype(F32).T
    raw_in = lax.psum_scatter(
        jnp.einsum("gd,gf->df", normed_all, d_in, preferred_element_type=F32).astype(BF16),
        "dp",
        scatter_dimension=0,
        tiled=True,
    ).astype(F32)
    in_sum = doubling_sum(jnp.sum(d_in, axis=0, dtype=F32)[None], "dp")[0]
    qkv_sum, up_sum = in_sum[:qkv_cols], in_sum[qkv_cols:]
    raw_qkv, raw_up = raw_in[:, :qkv_cols], raw_in[:, qkv_cols:]
    qkv_weight_grad = raw_qkv * gain1[:, None] + shift1[:, None] * qkv_sum[None]
    up_weight_grad = raw_up * gain2[:, None] + shift2[:, None] * up_sum[None]
    stats = jnp.stack(
        [
            jnp.sum(w_qkv * raw_qkv, axis=1),
            jnp.sum(w_qkv * qkv_sum[None], axis=1),
            jnp.sum(w_up * raw_up, axis=1),
            jnp.sum(w_up * up_sum[None], axis=1),
        ]
    )
    stats = doubling_gather(doubling_sum(stats, "tensor"), "dp")
    bias_grad = doubling_sum(
        doubling_sum(jnp.sum(cot_values, axis=0)[None], "tensor"), "dp"
    )[0]
    return (
        output,
        layer_input_gradient,
        stats[0],
        stats[1],
        stats[2],
        stats[3],
        qkv_weight_grad.reshape(shard_rows, 1, qkv_cols),
        qkv_sum.reshape(1, qkv_cols),
        out_grad[:HD],
        bias_grad,
        up_weight_grad,
        up_sum,
        out_grad[HD:],
        bias_grad,
    )


def solution(mesh):
    return jax.shard_map(
        body,
        mesh=mesh,
        in_specs=(
            P(("dp", "tensor"), None),
            P("dp", None),
            P(),
            P(),
            P(),
            P(),
            P("dp", "tensor", None),
            P("tensor", None),
            P("tensor", "dp"),
            P(),
            P("dp", "tensor"),
            P("tensor"),
            P("tensor", "dp"),
            P(),
            P(("dp", "tensor"), None),
        ),
        out_specs=(
            P(("dp", "tensor"), None),
            P(("dp", "tensor"), None),
            P(),
            P(),
            P(),
            P(),
            P("dp", "tensor", None),
            P("tensor", None),
            P("tensor", "dp"),
            P(),
            P("dp", "tensor"),
            P("tensor"),
            P("tensor", "dp"),
            P(),
        ),
        check_vma=False,
    )
```

```python
import functools
import math

import jax
import jax.numpy as jnp
from jax import lax
from jax.experimental import pallas as pl
from jax.experimental.pallas import tpu as pltpu
from jax.sharding import PartitionSpec as P

HD = 256
ROT = 64
LONGEST = 1024

NORM_EPS = 1e-05
MASK_FILL = -1e30
F32 = jnp.float32
BF16 = jnp.bfloat16
TILE = 256
VMEM_LIMIT = 50 * 1024 * 1024


def normalize(values):
    mean_val = jnp.mean(values, axis=-1, keepdims=True)
    centred = values - mean_val
    spread = jnp.mean(centred * centred, axis=-1, keepdims=True)
    inv_std = lax.rsqrt(spread + NORM_EPS)
    return (centred * inv_std, inv_std)


def segment_starts(segment):
    row_count = segment.shape[0]
    position_index = jnp.arange(row_count, dtype=jnp.int32)
    starts = jnp.concatenate([jnp.ones((1,), dtype=jnp.bool_), segment[1:] != segment[:-1]])
    return lax.cummax(jnp.where(starts, position_index, jnp.zeros_like(position_index)), axis=0)


def rotation_tables(position):
    half_dims = ROT // 2
    lane = jnp.arange(128, dtype=jnp.int32)
    inv_freq = 10000.0 ** (-2.0 * (lane % half_dims).astype(F32) / ROT)
    angles = position.astype(F32)[:, None] * inv_freq[None, :]
    turned = (lane < ROT)[None, :]
    sign = jnp.where(lane < half_dims, -1.0, 1.0).astype(F32)[None, :]
    cosine = jnp.where(turned, jnp.cos(angles), 1.0)
    sine = jnp.where(turned, sign * jnp.sin(angles), 0.0)
    return cosine, sine


def turn(values, cosine, sine):
    head = values[:, :128]
    lane = lax.broadcasted_iota(jnp.int32, head.shape, 1)
    partner = jnp.where(
        lane < ROT // 2, pltpu.roll(head, 128 - ROT // 2, 1), pltpu.roll(head, ROT // 2, 1)
    )
    return jnp.concatenate([head * cosine + partner * sine, values[:, 128:]], axis=1)


def tie(*values):
    return lax.optimization_barrier(values)


def after(value, *others):
    return lax.optimization_barrier((value,) + others)[0]


def nt_dot(a, b):
    return lax.dot_general(a, b, (((1,), (1,)), ((), ())), preferred_element_type=F32)


def tn_dot(a, b):
    return lax.dot_general(a, b, (((0,), (0,)), ((), ())), preferred_element_type=F32)


def params(*semantics):
    return pltpu.CompilerParams(dimension_semantics=semantics, vmem_limit_bytes=VMEM_LIMIT)


def project_kernel(pieces, bufs, *refs):
    ins, w_ref, bias_ref = refs[:pieces], refs[pieces], refs[pieces + 1]
    proj_ref, mixed_ref, slope_ref, rows_ref = refs[pieces + 2 + bufs :]
    j = pl.program_id(0)
    qkv_tiles = 3 * HD // TILE

    @pl.when(j == 0)
    def _():
        at = 0
        for ref in ins:
            rows_ref[at : at + ref.shape[0], :] = ref[...]
            at += ref.shape[0]

    out = jnp.dot(rows_ref[...], w_ref[...], preferred_element_type=F32) + bias_ref[...]

    @pl.when(j < qkv_tiles)
    def _():
        proj_ref[...] = out

    @pl.when(j >= qkv_tiles)
    def _():
        cdf = 0.5 * (1.0 + lax.erf(out * (1.0 / math.sqrt(2.0))))
        mixed_ref[...] = (out * cdf).astype(BF16)
        density = jnp.exp(-0.5 * out * out) * (1.0 / math.sqrt(2.0 * math.pi))
        slope_ref[...] = (cdf + out * density).astype(BF16)


def project(pieces, at, weight, bias, group_rows, bufs):
    width, cols = weight.shape
    count = sum(piece.shape[0] for piece in pieces)
    row = at // count
    qkv_tiles = 3 * HD // TILE
    hidden = cols - 3 * HD
    full = [pl.BlockSpec(piece.shape, lambda j: (0, 0)) for piece in pieces]
    any_spec = pl.BlockSpec(memory_space=pl.ANY)
    given = () if bufs is None else tuple(bufs)
    first = len(pieces) + 2
    return pl.pallas_call(
        functools.partial(project_kernel, len(pieces), len(given)),
        grid=(cols // TILE,),
        in_specs=full
        + [
            pl.BlockSpec((width, TILE), lambda j: (0, j)),
            pl.BlockSpec((1, TILE), lambda j: (0, j)),
        ]
        + [any_spec] * len(given),
        out_specs=[
            pl.BlockSpec((count, TILE), lambda j: (row, jnp.minimum(j, qkv_tiles - 1))),
            pl.BlockSpec(
                (count, TILE), lambda j: (row, HD // TILE + jnp.maximum(j - qkv_tiles, 0))
            ),
            pl.BlockSpec((count, TILE), lambda j: (row, jnp.maximum(j - qkv_tiles, 0))),
            pl.BlockSpec((count, width), lambda j: (row, 0)),
        ],
        out_shape=[
            jax.ShapeDtypeStruct((group_rows, 3 * HD), F32),
            jax.ShapeDtypeStruct((group_rows, HD + hidden), BF16),
            jax.ShapeDtypeStruct((group_rows, hidden), BF16),
            jax.ShapeDtypeStruct((group_rows, width), BF16),
        ],
        input_output_aliases={first + i: i for i in range(len(given))},
        compiler_params=params("arbitrary"),
        cost_estimate=pl.CostEstimate(
            flops=2 * count * width * cols,
            bytes_accessed=2 * (width * cols + 2 * count * width) + 8 * count * cols // 2,
            transcendentals=2 * count * hidden,
        ),
        name="project",
    )(*pieces, weight, bias, *given)


def back_kernel(pieces, bufs, *refs):
    ins, w_ref, slope_ref = refs[:pieces], refs[pieces], refs[pieces + 1]
    attn_ref, d_up_ref, rows_ref = refs[pieces + 2 + bufs :]
    j = pl.program_id(0)

    @pl.when(j == 0)
    def _():
        at = 0
        for ref in ins:
            rows_ref[at : at + ref.shape[0], :] = ref[...]
            at += ref.shape[0]

    out = nt_dot(rows_ref[...], w_ref[...])

    @pl.when(j == 0)
    def _():
        attn_ref[...] = out.astype(BF16)

    @pl.when(j > 0)
    def _():
        d_up_ref[...] = (out * slope_ref[...].astype(F32)).astype(BF16)


def back(pieces, at, weight, slope, bufs):
    cols, width = weight.shape
    group_rows, hidden = slope.shape
    count = sum(piece.shape[0] for piece in pieces)
    row = at // count
    full = [pl.BlockSpec(piece.shape, lambda j: (0, 0)) for piece in pieces]
    any_spec = pl.BlockSpec(memory_space=pl.ANY)
    given = () if bufs is None else tuple(bufs)
    first = len(pieces) + 2
    return pl.pallas_call(
        functools.partial(back_kernel, len(pieces), len(given)),
        grid=(cols // TILE,),
        in_specs=full
        + [
            pl.BlockSpec((TILE, width), lambda j: (j, 0)),
            pl.BlockSpec((count, TILE), lambda j: (row, jnp.maximum(j - 1, 0))),
        ]
        + [any_spec] * len(given),
        out_specs=[
            pl.BlockSpec((count, HD), lambda j: (row, 0)),
            pl.BlockSpec((count, TILE), lambda j: (row, jnp.maximum(j - 1, 0))),
            pl.BlockSpec((count, width), lambda j: (row, 0)),
        ],
        out_shape=[
            jax.ShapeDtypeStruct((group_rows, HD), BF16),
            jax.ShapeDtypeStruct((group_rows, hidden), BF16),
            jax.ShapeDtypeStruct((group_rows, width), BF16),
        ],
        input_output_aliases={first + i: i for i in range(len(given))},
        compiler_params=params("arbitrary"),
        cost_estimate=pl.CostEstimate(
            flops=2 * count * width * cols,
            bytes_accessed=2 * (width * cols + 2 * count * width + 3 * count * cols),
            transcendentals=0,
        ),
        name="back",
    )(*pieces, weight, slope, *given)


def window_mask(block, rows, start_ref):
    shape = (rows, LONGEST + rows)
    first_key = block * rows - LONGEST
    key_at = first_key + lax.broadcasted_iota(jnp.int32, shape, 1)
    query_at = block * rows + lax.broadcasted_iota(jnp.int32, shape, 0)
    return (key_at >= start_ref[...]) & (key_at <= query_at)


def attend_kernel(
    rows, slot_ref, proj_ref, cos_ref, sin_ref, start_ref, _, mixed_ref, q_ref, k_ref, v_ref, lse_ref
):
    block = pl.program_id(0)

    @pl.when(block == 0)
    def _():
        k_ref[:LONGEST, :] = jnp.zeros((LONGEST, HD), BF16)
        v_ref[:LONGEST, :] = jnp.zeros((LONGEST, HD), BF16)
        k_ref[LONGEST + rows :, :] = jnp.zeros((k_ref.shape[0] - LONGEST - rows, HD), BF16)
        v_ref[LONGEST + rows :, :] = jnp.zeros((k_ref.shape[0] - LONGEST - rows, HD), BF16)

    cosine, sine = cos_ref[...], sin_ref[...]
    query = turn(proj_ref[:, :HD], cosine, sine).astype(BF16)
    at = pl.multiple_of(block * rows, rows)
    q_ref[...] = query
    k_ref[pl.ds(LONGEST + at, rows), :] = turn(proj_ref[:, HD : 2 * HD], cosine, sine).astype(BF16)
    v_ref[pl.ds(LONGEST + at, rows), :] = proj_ref[:, 2 * HD :].astype(BF16)
    window = pl.ds(at, LONGEST + rows)
    scores = nt_dot(query, k_ref[window, :]) * (1.0 / math.sqrt(HD))
    scores = jnp.where(window_mask(block, rows, start_ref), scores, MASK_FILL)
    top = jnp.max(scores, axis=1, keepdims=True)
    weights = jnp.exp(scores - top)
    total = jnp.sum(weights, axis=1, keepdims=True)
    low = (weights * (1.0 / total)).astype(BF16)
    mixed_ref[...] = jnp.dot(low, v_ref[window, :], preferred_element_type=F32).astype(BF16)
    lse_ref[...] = top + jnp.log(total)


def attend(slots, proj, cosine, sine, start, mixed, rows):
    group_rows = proj.shape[0]
    padded = group_rows + LONGEST
    by_slot = lambda i, slot: (slot[i], 0)
    in_order = lambda i, slot: (i, 0)
    whole = lambda i, slot: (0, 0)
    return pl.pallas_call(
        functools.partial(attend_kernel, rows),
        grid_spec=pltpu.PrefetchScalarGridSpec(
            num_scalar_prefetch=1,
            grid=(group_rows // rows,),
            in_specs=[
                pl.BlockSpec((rows, 3 * HD), by_slot),
                pl.BlockSpec((rows, 128), in_order),
                pl.BlockSpec((rows, 128), in_order),
                pl.BlockSpec((rows, 1), in_order),
                pl.BlockSpec(memory_space=pl.ANY),
            ],
            out_specs=[
                pl.BlockSpec((rows, HD), by_slot),
                pl.BlockSpec((rows, HD), in_order),
                pl.BlockSpec((padded, HD), whole),
                pl.BlockSpec((padded, HD), whole),
                pl.BlockSpec((rows, 1), in_order),
            ],
        ),
        out_shape=[
            jax.ShapeDtypeStruct(mixed.shape, BF16),
            jax.ShapeDtypeStruct((group_rows, HD), BF16),
            jax.ShapeDtypeStruct((padded, HD), BF16),
            jax.ShapeDtypeStruct((padded, HD), BF16),
            jax.ShapeDtypeStruct((group_rows, 1), F32),
        ],
        input_output_aliases={5: 0},
        compiler_params=params("arbitrary"),
        cost_estimate=pl.CostEstimate(
            flops=4 * group_rows * (LONGEST + rows) * HD,
            bytes_accessed=group_rows * HD * 22,
            transcendentals=group_rows * (LONGEST + rows),
        ),
        name="attend",
    )(slots, proj, cosine, sine, start, mixed)


def attend_back_kernel(
    rows, slot_ref, d_attn_ref, q_ref, k_ref, v_ref, lse_ref, start_ref, cos_ref, sin_ref,
    d_proj_ref, dk_ref, dv_ref,
):
    block = pl.program_id(0)
    blocks = pl.num_programs(0)
    scale = 1.0 / math.sqrt(HD)

    @pl.when(block == 0)
    def _():
        dk_ref[...] = jnp.zeros_like(dk_ref)
        dv_ref[...] = jnp.zeros_like(dv_ref)

    at = pl.multiple_of(block * rows, rows)
    window = pl.ds(at, LONGEST + rows)
    query, d_attn = q_ref[...], d_attn_ref[...]
    keys = k_ref[window, :]
    scores = nt_dot(query, keys) * scale
    mask = window_mask(block, rows, start_ref)
    probs = jnp.exp(jnp.where(mask, scores - lse_ref[...], MASK_FILL))
    d_probs = nt_dot(d_attn, v_ref[window, :])
    inner = jnp.sum(probs * d_probs, axis=1, keepdims=True)
    d_scores = (probs * (d_probs - inner)).astype(BF16)
    d_query = jnp.dot(d_scores, keys, preferred_element_type=F32) * scale
    dk_ref[window, :] += tn_dot(d_scores, query)
    dv_ref[window, :] += tn_dot(probs.astype(BF16), d_attn)
    here = pl.ds(at, rows)
    slot = pl.ds(pl.multiple_of(slot_ref[block] * rows, rows), rows)
    d_proj_ref[slot, :HD] = turn(d_query, cos_ref[here, :], -sin_ref[here, :]).astype(BF16)

    @pl.when(block == blocks - 1)
    def _():
        def finish(i, carry):
            own = pl.ds(pl.multiple_of(i * rows, rows), rows)
            padded = pl.ds(pl.multiple_of(i * rows, rows) + LONGEST, rows)
            to = pl.ds(pl.multiple_of(slot_ref[i] * rows, rows), rows)
            d_key = turn(dk_ref[padded, :] * scale, cos_ref[own, :], -sin_ref[own, :])
            d_proj_ref[to, HD : 2 * HD] = d_key.astype(BF16)
            d_proj_ref[to, 2 * HD :] = dv_ref[padded, :].astype(BF16)
            return carry

        lax.fori_loop(0, blocks, finish, 0)


def attend_back(slots, d_attn, query, keys, values, lse, start, cosine, sine, rows):
    group_rows = query.shape[0]
    padded = keys.shape[0]
    by_slot = lambda i, slot: (slot[i], 0)
    in_order = lambda i, slot: (i, 0)
    whole = lambda i, slot: (0, 0)
    return pl.pallas_call(
        functools.partial(attend_back_kernel, rows),
        grid_spec=pltpu.PrefetchScalarGridSpec(
            num_scalar_prefetch=1,
            grid=(group_rows // rows,),
            in_specs=[
                pl.BlockSpec((rows, HD), by_slot),
                pl.BlockSpec((rows, HD), in_order),
                pl.BlockSpec((padded, HD), whole),
                pl.BlockSpec((padded, HD), whole),
                pl.BlockSpec((rows, 1), in_order),
                pl.BlockSpec((rows, 1), in_order),
                pl.BlockSpec((group_rows, 128), whole),
                pl.BlockSpec((group_rows, 128), whole),
            ],
            out_specs=pl.BlockSpec((group_rows, 3 * HD), whole),
            scratch_shapes=[pltpu.VMEM((padded, HD), F32), pltpu.VMEM((padded, HD), F32)],
        ),
        out_shape=jax.ShapeDtypeStruct((group_rows, 3 * HD), BF16),
        compiler_params=params("arbitrary"),
        cost_estimate=pl.CostEstimate(
            flops=10 * group_rows * (LONGEST + rows) * HD,
            bytes_accessed=group_rows * HD * 20,
            transcendentals=group_rows * (LONGEST + rows),
        ),
        name="attend_back",
    )(slots, d_attn, query, keys, values, lse, start, cosine, sine)


class Ring:
    def __init__(self, axis):
        self.axis = axis
        size = lax.axis_size(axis)
        order = list(range(0, size, 2)) + list(range(size - 1, 0, -2))
        place = [order.index(i) for i in range(size)]
        self.size, self.far = size, size // 2
        self.up_pairs = [(order[i], order[(i + 1) % size]) for i in range(size)]
        self.down_pairs = [(order[i], order[(i - 1) % size]) for i in range(size)]
        slot_of = [0] * size
        for offset in range(size):
            slot_of[offset] = self.slot(offset)
        here = jnp.array(place, jnp.int32)[lax.axis_index(axis)]
        offsets = (jnp.array(place, jnp.int32) - here + size) % size
        self.slots = jnp.array(slot_of, jnp.int32)[offsets]

    def slot(self, offset):
        offset %= self.size
        if offset == 0:
            return 0
        if offset == self.far:
            return 1
        return 2 * offset + 1 if offset < self.far else 2 * (self.size - offset)

    def up(self, value):
        return lax.ppermute(value, self.axis, self.up_pairs)

    def down(self, value):
        return lax.ppermute(value, self.axis, self.down_pairs)


def doubling_sum(value, axis):
    size = lax.axis_size(axis)
    step = 1
    while step < size:
        value = value + lax.ppermute(value, axis, [(i, i ^ step) for i in range(size)])
        step *= 2
    return value


def doubling_gather(value, axis):
    size = lax.axis_size(axis)
    me = lax.axis_index(axis)
    step = 1
    while step < size:
        other = lax.ppermute(value, axis, [(i, i ^ step) for i in range(size)])
        upper = (me & step) != 0
        value = jnp.where(
            upper,
            jnp.concatenate([other, value], axis=1),
            jnp.concatenate([value, other], axis=1),
        )
        step *= 2
    return value


def body(
    tokens,
    segment_ids,
    first_gain,
    first_shift,
    second_gain,
    second_shift,
    qkv_weight,
    qkv_bias,
    out_weight,
    out_bias,
    up_projection_weight,
    up_bias,
    down_weight,
    down_bias,
    cotangent,
):
    rows, width = tokens.shape
    qkv_cols = 3 * HD
    segment = segment_ids[0]
    group_rows = segment.shape[0]
    ring = Ring("tensor")
    far = ring.far
    half = rows // 2
    shard_rows = qkv_weight.shape[0]
    dp_start = lax.axis_index("dp") * shard_rows

    x_values = tokens.astype(F32)
    normed, inv_std = normalize(x_values)
    normed_low = normed.astype(BF16)

    w_qkv = qkv_weight.reshape(shard_rows, qkv_cols).astype(F32)
    w_up = up_projection_weight.astype(F32)

    def shard(vector):
        return lax.dynamic_slice(vector, (dp_start,), (shard_rows,)).astype(F32)

    gain1, gain2 = shard(first_gain), shard(second_gain)
    shift1, shift2 = shard(first_shift), shard(second_shift)
    scaled = jnp.concatenate(
        [w_qkv * gain1[:, None], w_up * gain2[:, None]], axis=1
    ).astype(BF16)
    w_in = lax.all_gather(scaled, "dp", axis=0, tiled=True)
    shift_part = jnp.concatenate(
        [jnp.sum(w_qkv * shift1[:, None], axis=0), jnp.sum(w_up * shift2[:, None], axis=0)]
    )
    in_bias = doubling_sum(shift_part[None], "dp") + jnp.concatenate(
        [qkv_bias.reshape(-1), up_bias]
    ).astype(F32)[None]
    w_out = lax.all_gather(
        jnp.concatenate([out_weight, down_weight], axis=0), "dp", axis=1, tiled=True
    )
    start = segment_starts(segment)
    cosine, sine = rotation_tables(jnp.arange(group_rows, dtype=jnp.int32) - start)
    start = start[:, None]

    def row_of(offset):
        return ring.slot(offset) * rows

    def pair(step):
        return row_of(-step)

    up1, down1 = ring.up(normed_low), ring.down(normed_low)
    up2, down2 = ring.up(up1), ring.down(down1)
    up3, down3 = ring.up(up2), ring.down(down2)
    own = after(normed_low, up2, down2)
    bufs = project([own], 0, w_in, in_bias, group_rows, None)
    bufs = project([up1, down1], pair(1), w_in, in_bias, group_rows, bufs)
    up3, down3, *bufs = tie(up3, down3, *bufs)

    cot_own = after(cotangent, up3, down3)
    far_up, far_down = ring.up(up3[:half]), ring.down(down3[half:])
    cot_up1, cot_down1 = ring.up(cot_own), ring.down(cot_own)
    bufs = project([up2, down2], pair(2), w_in, in_bias, group_rows, bufs)
    bufs = project([up3, down3], pair(3), w_in, in_bias, group_rows, bufs)
    far_up, far_down, cot_up1, cot_down1, *bufs = tie(far_up, far_down, cot_up1, cot_down1, *bufs)

    cot_up2, cot_down2 = ring.up(cot_up1), ring.down(cot_down1)
    bufs = project([far_up, far_down], rows, w_in, in_bias, group_rows, bufs)
    proj, mixed, slope, normed_all = bufs
    mixed, query, keys, values, lse = attend(ring.slots, proj, cosine, sine, start, mixed, rows)
    cot_up2, cot_down2, mixed, slope = tie(cot_up2, cot_down2, mixed, slope)

    cot_up3, cot_down3 = ring.up(cot_up2), ring.down(cot_down2)
    grads = back([cot_own], 0, w_out, slope, None)
    grads = back([cot_up1, cot_down1], pair(1), w_out, slope, grads)
    grads = back([cot_up2, cot_down2], pair(2), w_out, slope, grads)
    cot_up3, cot_down3, mixed, *grads = tie(cot_up3, cot_down3, mixed, *grads)

    cot_far_up, cot_far_down = ring.up(cot_up3[:half]), ring.down(cot_down3[half:])

    def out_part(first, count):
        return jnp.dot(mixed[first : first + count], w_out, preferred_element_type=F32)

    def first_step(part):
        at = row_of(far)
        return (
            ring.up(part(at, half).astype(BF16)),
            ring.down(part(at + half, half).astype(BF16)),
        )

    def next_step(part, step, moving_up, moving_down):
        moving_up, moving_down = moving_up.astype(F32), moving_down.astype(F32)
        if step == 1:
            moving_up = jnp.pad(moving_up, ((0, rows - half), (0, 0)))
            moving_down = jnp.pad(moving_down, ((half, 0), (0, 0)))
        up = part(row_of(far - step), rows) + moving_up
        down = part(row_of(step - far), rows) + moving_down
        return ring.up(up.astype(BF16)), ring.down(down.astype(BF16))

    out_up, out_down = first_step(out_part)
    grads = back([cot_up3, cot_down3], pair(3), w_out, slope, grads)
    cot_far_up, cot_far_down, out_up, out_down, *grads = tie(
        cot_far_up, cot_far_down, out_up, out_down, *grads
    )

    out_up, out_down = next_step(out_part, 1, out_up, out_down)
    grads = back([cot_far_up, cot_far_down], rows, w_out, slope, grads)
    d_attn, d_up, cot_all = grads
    d_proj = attend_back(
        ring.slots, d_attn, query, keys, values, lse, start, cosine, sine, rows
    )
    out_up, out_down, d_proj, d_up, cot_all = tie(out_up, out_down, d_proj, d_up, cot_all)

    out_up, out_down = next_step(out_part, 2, out_up, out_down)
    raw_up = tn_dot(normed_all, d_up).astype(BF16)
    raw_qkv = tn_dot(normed_all, d_proj).astype(BF16)
    out_up, out_down, raw_up, raw_qkv = tie(out_up, out_down, raw_up, raw_qkv)
    raw_up = lax.psum_scatter(raw_up, "dp", scatter_dimension=0, tiled=True)
    raw_qkv = lax.psum_scatter(raw_qkv, "dp", scatter_dimension=0, tiled=True)
    in_sum = jnp.concatenate(
        [jnp.sum(d_proj, axis=0, dtype=F32), jnp.sum(d_up, axis=0, dtype=F32)]
    )
    in_sum = doubling_sum(in_sum[None], "dp")

    out_up, out_down = next_step(out_part, 3, out_up, out_down)

    def grad_part(first, count):
        return nt_dot(d_proj[first : first + count], w_in[:, :qkv_cols]) + nt_dot(
            d_up[first : first + count], w_in[:, qkv_cols:]
        )

    grad_up, grad_down = first_step(grad_part)
    out_grad = tn_dot(cot_all, mixed).astype(BF16)
    out_up, out_down, grad_up, grad_down, out_grad = tie(
        out_up, out_down, grad_up, grad_down, out_grad
    )
    out_grad = lax.psum_scatter(out_grad, "dp", scatter_dimension=0, tiled=True)

    grad_up, grad_down = next_step(grad_part, 1, grad_up, grad_down)
    summed = out_part(0, rows) + out_up.astype(F32) + out_down.astype(F32)
    output = (x_values + out_bias.astype(F32) + down_bias.astype(F32) + summed).astype(BF16)
    grad_up, grad_down, output = tie(grad_up, grad_down, output)
    grad_up, grad_down = next_step(grad_part, 2, grad_up, grad_down)
    grad_up, grad_down = next_step(grad_part, 3, grad_up, grad_down)
    grad_normed = grad_part(0, rows) + grad_up.astype(F32) + grad_down.astype(F32)
    cot_values = cotangent.astype(F32)
    layer_input_gradient = cot_values + inv_std * (
        grad_normed
        - jnp.mean(grad_normed, axis=1, keepdims=True)
        - normed * jnp.mean(grad_normed * normed, axis=1, keepdims=True)
    )

    out_grad = out_grad.astype(F32).T
    raw_qkv, raw_up = raw_qkv.astype(F32), raw_up.astype(F32)
    qkv_sum, up_sum = in_sum[:, :qkv_cols], in_sum[:, qkv_cols:]
    qkv_weight_grad = raw_qkv * gain1[:, None] + shift1[:, None] * qkv_sum
    up_weight_grad = raw_up * gain2[:, None] + shift2[:, None] * up_sum
    stats = jnp.stack(
        [
            jnp.sum(w_qkv * raw_qkv, axis=1),
            jnp.sum(w_qkv * qkv_sum, axis=1),
            jnp.sum(w_up * raw_up, axis=1),
            jnp.sum(w_up * up_sum, axis=1),
        ]
    )
    stats = doubling_gather(doubling_sum(stats, "tensor"), "dp")
    bias_grad = doubling_sum(
        doubling_sum(jnp.sum(cot_values, axis=0)[None], "tensor"), "dp"
    )[0]
    return (
        output,
        layer_input_gradient,
        stats[0],
        stats[1],
        stats[2],
        stats[3],
        qkv_weight_grad.reshape(shard_rows, 1, qkv_cols),
        qkv_sum,
        out_grad[:HD],
        bias_grad,
        up_weight_grad,
        up_sum[0],
        out_grad[HD:],
        bias_grad,
    )


def solution(mesh):
    return jax.shard_map(
        body,
        mesh=mesh,
        in_specs=(
            P(("dp", "tensor"), None),
            P("dp", None),
            P(),
            P(),
            P(),
            P(),
            P("dp", "tensor", None),
            P("tensor", None),
            P("tensor", "dp"),
            P(),
            P("dp", "tensor"),
            P("tensor"),
            P("tensor", "dp"),
            P(),
            P(("dp", "tensor"), None),
        ),
        out_specs=(
            P(("dp", "tensor"), None),
            P(("dp", "tensor"), None),
            P(),
            P(),
            P(),
            P(),
            P("dp", "tensor", None),
            P("tensor", None),
            P("tensor", "dp"),
            P(),
            P("dp", "tensor"),
            P("tensor"),
            P("tensor", "dp"),
            P(),
        ),
        check_vma=False,
    )
```

```python
import functools
import math

import jax
import jax.numpy as jnp
from jax import lax
from jax.experimental import pallas as pl
from jax.experimental.pallas import tpu as pltpu
from jax.sharding import PartitionSpec as P

HD = 256
ROT = 64
LONGEST = 1024

NORM_EPS = 1e-05
MASK_FILL = -1e30
F32 = jnp.float32
BF16 = jnp.bfloat16
TILE = 256
MIB = 1024 * 1024
PROJECT_MIB = 36
BACK_MIB = 36
ATTEND_MIB = 28
ATTEND_BACK_MIB = 40


def normalize(values):
    mean_val = jnp.mean(values, axis=-1, keepdims=True)
    centred = values - mean_val
    spread = jnp.mean(centred * centred, axis=-1, keepdims=True)
    inv_std = lax.rsqrt(spread + NORM_EPS)
    return (centred * inv_std, inv_std)


def segment_starts(segment):
    row_count = segment.shape[0]
    position_index = jnp.arange(row_count, dtype=jnp.int32)
    starts = jnp.concatenate([jnp.ones((1,), dtype=jnp.bool_), segment[1:] != segment[:-1]])
    return lax.cummax(jnp.where(starts, position_index, jnp.zeros_like(position_index)), axis=0)


def rotation_tables(position):
    half_dims = ROT // 2
    lane = jnp.arange(128, dtype=jnp.int32)
    inv_freq = 10000.0 ** (-2.0 * (lane % half_dims).astype(F32) / ROT)
    angles = position.astype(F32)[:, None] * inv_freq[None, :]
    turned = (lane < ROT)[None, :]
    sign = jnp.where(lane < half_dims, -1.0, 1.0).astype(F32)[None, :]
    cosine = jnp.where(turned, jnp.cos(angles), 1.0)
    sine = jnp.where(turned, sign * jnp.sin(angles), 0.0)
    return cosine, sine


def turn(values, cosine, sine):
    head = values[:, :128]
    lane = lax.broadcasted_iota(jnp.int32, head.shape, 1)
    partner = jnp.where(
        lane < ROT // 2, pltpu.roll(head, 128 - ROT // 2, 1), pltpu.roll(head, ROT // 2, 1)
    )
    return jnp.concatenate([head * cosine + partner * sine, values[:, 128:]], axis=1)


def tie(*values):
    return lax.optimization_barrier(values)


def after(value, *others):
    return lax.optimization_barrier((value, others))[0]


def nt_dot(a, b):
    return lax.dot_general(a, b, (((1,), (1,)), ((), ())), preferred_element_type=F32)


def tn_dot(a, b):
    return lax.dot_general(a, b, (((0,), (0,)), ((), ())), preferred_element_type=F32)


def params(mib):
    return pltpu.CompilerParams(dimension_semantics=("arbitrary",), vmem_limit_bytes=mib * MIB)


def in_hbm(*values):
    return [pltpu.with_memory_space_constraint(value, pltpu.HBM) for value in values]


def fill(ins, rows_ref):
    at = 0
    for ref in ins:
        rows_ref[at : at + ref.shape[0], :] = ref[...]
        at += ref.shape[0]


def project_kernel(pieces, qkv_tiles, refs):
    w_ref, bias_ref = refs[pieces], refs[pieces + 1]
    proj_ref, mixed_ref, slope_ref, rows_ref = refs[-4:]
    j = pl.program_id(0)

    @pl.when(j == 0)
    def _():
        fill(refs[:pieces], rows_ref)

    def product():
        return jnp.dot(rows_ref[...], w_ref[...], preferred_element_type=F32) + bias_ref[...]

    @pl.when(j < qkv_tiles)
    def _():
        proj_ref[...] = product()

    @pl.when(j >= qkv_tiles)
    def _():
        out = product()
        cdf = 0.5 * (1.0 + lax.erf(out * (1.0 / math.sqrt(2.0))))
        mixed_ref[...] = (out * cdf).astype(BF16)
        density = jnp.exp(-0.5 * out * out) * (1.0 / math.sqrt(2.0 * math.pi))
        slope_ref[...] = (cdf + out * density).astype(BF16)


def aligned(col):
    return pl.multiple_of(col, TILE)


def at_element(rows, cols, index):
    return pl.BlockSpec((pl.Element(rows), pl.Element(cols)), index)


def in_place(kernel, grid, pieces, row, extra, extra_specs, bufs, buf_types, out_specs, mib, cost, name):
    given = () if bufs is None else tuple(bufs)
    first = len(pieces) + len(extra)
    return pl.pallas_call(
        lambda *refs: kernel(refs),
        grid=grid,
        in_specs=[pl.BlockSpec(piece.shape, lambda j: (0, 0)) for piece in pieces]
        + extra_specs
        + [pl.BlockSpec(memory_space=pltpu.HBM)] * len(given),
        out_specs=out_specs,
        out_shape=[pltpu.HBM(shape, dtype) for shape, dtype in buf_types],
        input_output_aliases={first + i: i for i in range(len(given))},
        compiler_params=params(mib),
        cost_estimate=cost,
        name=name,
    )(*in_hbm(*pieces, *extra), *given)


def project(pieces, row, weight, bias, group_rows, bufs):
    width, cols = weight.shape
    count = sum(piece.shape[0] for piece in pieces)
    qkv_tiles = 3 * HD // TILE
    hidden = cols - 3 * HD
    up_tile = lambda j: jnp.maximum(j - qkv_tiles, 0) * TILE
    return in_place(
        functools.partial(project_kernel, len(pieces), qkv_tiles),
        (cols // TILE,),
        pieces,
        row,
        (weight, bias),
        [
            pl.BlockSpec((width, TILE), lambda j: (0, j)),
            pl.BlockSpec((1, TILE), lambda j: (0, j)),
        ],
        bufs,
        [
            ((group_rows, 3 * HD), F32),
            ((group_rows, HD + hidden), BF16),
            ((group_rows, hidden), BF16),
            ((group_rows, width), BF16),
        ],
        [
            at_element(count, TILE, lambda j: (row, aligned(jnp.minimum(j, qkv_tiles - 1) * TILE))),
            at_element(count, TILE, lambda j: (row, aligned(HD + up_tile(j)))),
            at_element(count, TILE, lambda j: (row, aligned(up_tile(j)))),
            at_element(count, width, lambda j: (row, 0)),
        ],
        PROJECT_MIB,
        pl.CostEstimate(
            flops=2 * count * width * cols,
            bytes_accessed=2 * (width * cols + 2 * count * width) + 8 * count * cols // 2,
            transcendentals=2 * count * hidden,
        ),
        "project",
    )


def back_kernel(pieces, refs):
    w_ref, slope_ref = refs[pieces], refs[pieces + 1]
    attn_ref, d_in_ref, rows_ref = refs[-3:]
    j = pl.program_id(0)

    @pl.when(j == 0)
    def _():
        fill(refs[:pieces], rows_ref)

    out = jnp.dot(rows_ref[...], w_ref[...], preferred_element_type=F32)

    @pl.when(j == 0)
    def _():
        attn_ref[...] = out.astype(BF16)

    @pl.when(j > 0)
    def _():
        d_in_ref[...] = (out * slope_ref[...].astype(F32)).astype(BF16)


def back(pieces, row, weight, slope, bufs):
    width, cols = weight.shape
    group_rows, hidden = slope.shape
    count = sum(piece.shape[0] for piece in pieces)
    up_tile = lambda j: jnp.maximum(j - 1, 0) * TILE
    return in_place(
        functools.partial(back_kernel, len(pieces)),
        (cols // TILE,),
        pieces,
        row,
        (weight, slope),
        [
            pl.BlockSpec((width, TILE), lambda j: (0, j)),
            at_element(count, TILE, lambda j: (row, aligned(up_tile(j)))),
        ],
        bufs,
        [
            ((group_rows, HD), BF16),
            ((group_rows, 3 * HD + hidden), BF16),
            ((group_rows, width), BF16),
        ],
        [
            at_element(count, HD, lambda j: (row, 0)),
            at_element(count, TILE, lambda j: (row, aligned(3 * HD + up_tile(j)))),
            at_element(count, width, lambda j: (row, 0)),
        ],
        BACK_MIB,
        pl.CostEstimate(
            flops=2 * count * width * cols,
            bytes_accessed=2 * (width * cols + 2 * count * width + 3 * count * cols),
            transcendentals=0,
        ),
        "back",
    )


def window_mask(block, rows, count, start_ref):
    shape = (rows, count * rows)
    key_at = (block - count + 1) * rows + lax.broadcasted_iota(jnp.int32, shape, 1)
    query_at = block * rows + lax.broadcasted_iota(jnp.int32, shape, 0)
    return (key_at >= start_ref[...]) & (key_at <= query_at)


def by_count(reach_ref, rows, visit):
    block = pl.program_id(0)
    for count in range(1, LONGEST // rows + 2):

        @pl.when(reach_ref[block] == count)
        def _():
            first = pl.multiple_of((block - count + 1) * rows, rows)
            visit(count, pl.ds(first, count * rows))


def attend_kernel(
    rows, slot_ref, reach_ref, proj_ref, cos_ref, sin_ref, start_ref, _,
    mixed_ref, q_ref, k_ref, v_ref, lse_ref,
):
    block = pl.program_id(0)
    cosine, sine = cos_ref[...], sin_ref[...]
    here = pl.ds(pl.multiple_of(block * rows, rows), rows)
    q_ref[...] = turn(proj_ref[:, :HD], cosine, sine).astype(BF16)
    k_ref[here, :] = turn(proj_ref[:, HD : 2 * HD], cosine, sine).astype(BF16)
    v_ref[here, :] = proj_ref[:, 2 * HD :].astype(BF16)

    def visit(count, window):
        scores = nt_dot(q_ref[...], k_ref[window, :]) * (1.0 / math.sqrt(HD))
        scores = jnp.where(window_mask(block, rows, count, start_ref), scores, MASK_FILL)
        top = jnp.max(scores, axis=1, keepdims=True)
        weights = jnp.exp(scores - top)
        total = jnp.sum(weights, axis=1, keepdims=True)
        low = (weights * (1.0 / total)).astype(BF16)
        mixed_ref[...] = jnp.dot(low, v_ref[window, :], preferred_element_type=F32).astype(BF16)
        lse_ref[...] = top + jnp.log(total)

    by_count(reach_ref, rows, visit)


def attend(slots, reach, proj, cosine, sine, start, mixed, rows):
    group_rows = proj.shape[0]
    by_slot = lambda i, slot, reach: (slot[i], 0)
    in_order = lambda i, slot, reach: (i, 0)
    whole = lambda i, slot, reach: (0, 0)
    return pl.pallas_call(
        functools.partial(attend_kernel, rows),
        grid_spec=pltpu.PrefetchScalarGridSpec(
            num_scalar_prefetch=2,
            grid=(group_rows // rows,),
            in_specs=[
                pl.BlockSpec((rows, 3 * HD), by_slot),
                pl.BlockSpec((rows, 128), in_order),
                pl.BlockSpec((rows, 128), in_order),
                pl.BlockSpec((rows, 1), in_order),
                pl.BlockSpec(memory_space=pltpu.HBM),
            ],
            out_specs=[
                pl.BlockSpec((rows, HD), by_slot),
                pl.BlockSpec((rows, HD), in_order),
                pl.BlockSpec((group_rows, HD), whole),
                pl.BlockSpec((group_rows, HD), whole),
                pl.BlockSpec((rows, 1), in_order),
            ],
        ),
        out_shape=[
            pltpu.HBM(mixed.shape, BF16),
            pltpu.HBM((group_rows, HD), BF16),
            pltpu.HBM((group_rows, HD), BF16),
            pltpu.HBM((group_rows, HD), BF16),
            pltpu.HBM((group_rows, 1), F32),
        ],
        input_output_aliases={6: 0},
        compiler_params=params(ATTEND_MIB),
        cost_estimate=pl.CostEstimate(
            flops=4 * group_rows * LONGEST * HD,
            bytes_accessed=group_rows * HD * 22,
            transcendentals=group_rows * LONGEST,
        ),
        name="attend",
    )(slots, reach, *in_hbm(proj, cosine, sine, start), mixed)


def attend_back_kernel(
    rows, slot_ref, reach_ref, d_attn_ref, q_ref, k_ref, v_ref, lse_ref, start_ref, cos_ref, sin_ref,
    _, d_proj_ref, dk_ref, dv_ref,
):
    block = pl.program_id(0)
    blocks = pl.num_programs(0)
    scale = 1.0 / math.sqrt(HD)
    here = pl.ds(pl.multiple_of(block * rows, rows), rows)
    slot = pl.ds(pl.multiple_of(slot_ref[block] * rows, rows), rows)
    dk_ref[here, :] = jnp.zeros((rows, HD), F32)
    dv_ref[here, :] = jnp.zeros((rows, HD), F32)

    def visit(count, window):
        query, d_attn, keys = q_ref[...], d_attn_ref[...], k_ref[window, :]
        scores = nt_dot(query, keys) * scale
        mask = window_mask(block, rows, count, start_ref)
        probs = jnp.exp(jnp.where(mask, scores - lse_ref[...], MASK_FILL))
        d_probs = nt_dot(d_attn, v_ref[window, :])
        inner = jnp.sum(probs * d_probs, axis=1, keepdims=True)
        d_scores = (probs * (d_probs - inner)).astype(BF16)
        d_query = jnp.dot(d_scores, keys, preferred_element_type=F32) * scale
        dk_ref[window, :] += tn_dot(d_scores, query)
        dv_ref[window, :] += tn_dot(probs.astype(BF16), d_attn)
        d_proj_ref[slot, :HD] = turn(d_query, cos_ref[here, :], -sin_ref[here, :]).astype(BF16)

    by_count(reach_ref, rows, visit)

    @pl.when(block == blocks - 1)
    def _():
        def finish(i, carry):
            own = pl.ds(pl.multiple_of(i * rows, rows), rows)
            to = pl.ds(pl.multiple_of(slot_ref[i] * rows, rows), rows)
            d_key = turn(dk_ref[own, :] * scale, cos_ref[own, :], -sin_ref[own, :])
            d_proj_ref[to, HD : 2 * HD] = d_key.astype(BF16)
            d_proj_ref[to, 2 * HD :] = dv_ref[own, :].astype(BF16)
            return carry

        lax.fori_loop(0, blocks, finish, 0)


def attend_back(slots, reach, d_attn, query, keys, values, lse, start, cosine, sine, d_in, rows):
    group_rows = query.shape[0]
    by_slot = lambda i, slot, reach: (slot[i], 0)
    in_order = lambda i, slot, reach: (i, 0)
    whole = lambda i, slot, reach: (0, 0)
    return pl.pallas_call(
        functools.partial(attend_back_kernel, rows),
        grid_spec=pltpu.PrefetchScalarGridSpec(
            num_scalar_prefetch=2,
            grid=(group_rows // rows,),
            in_specs=[
                pl.BlockSpec((rows, HD), by_slot),
                pl.BlockSpec((rows, HD), in_order),
                pl.BlockSpec((group_rows, HD), whole),
                pl.BlockSpec((group_rows, HD), whole),
                pl.BlockSpec((rows, 1), in_order),
                pl.BlockSpec((rows, 1), in_order),
                pl.BlockSpec((group_rows, 128), whole),
                pl.BlockSpec((group_rows, 128), whole),
                pl.BlockSpec(memory_space=pltpu.HBM),
            ],
            out_specs=pl.BlockSpec((group_rows, 3 * HD), whole),
            scratch_shapes=[pltpu.VMEM((group_rows, HD), F32), pltpu.VMEM((group_rows, HD), F32)],
        ),
        out_shape=pltpu.HBM(d_in.shape, BF16),
        input_output_aliases={10: 0},
        compiler_params=params(ATTEND_BACK_MIB),
        cost_estimate=pl.CostEstimate(
            flops=10 * group_rows * LONGEST * HD,
            bytes_accessed=group_rows * HD * 20,
            transcendentals=group_rows * LONGEST,
        ),
        name="attend_back",
    )(slots, reach, *in_hbm(d_attn, query, keys, values, lse, start, cosine, sine), d_in)


class Ring:
    def __init__(self, axis):
        self.axis = axis
        size = lax.axis_size(axis)
        order = list(range(0, size, 2)) + list(range(size - 1, 0, -2))
        place = [order.index(i) for i in range(size)]
        self.size, self.far = size, size // 2
        self.up_pairs = [(order[i], order[(i + 1) % size]) for i in range(size)]
        self.down_pairs = [(order[i], order[(i - 1) % size]) for i in range(size)]
        slot_of = [0] * size
        for offset in range(size):
            slot_of[offset] = self.slot(offset)
        here = jnp.array(place, jnp.int32)[lax.axis_index(axis)]
        offsets = (jnp.array(place, jnp.int32) - here + size) % size
        self.slots = jnp.array(slot_of, jnp.int32)[offsets]

    def slot(self, offset):
        offset %= self.size
        if offset == 0:
            return 0
        if offset == self.far:
            return self.size - 1
        return 2 * offset if offset < self.far else 2 * (self.size - offset) - 1

    def up(self, value):
        return lax.ppermute(value, self.axis, self.up_pairs)

    def down(self, value):
        return lax.ppermute(value, self.axis, self.down_pairs)


def swap(value, axis, step):
    return lax.ppermute(value, axis, [(i, i ^ step) for i in range(lax.axis_size(axis))])


def from_all(value, axis):
    return [value] + [swap(value, axis, step) for step in range(1, lax.axis_size(axis))]


def tree_sum(values):
    while len(values) > 1:
        values = [a + b for a, b in zip(values[0::2], values[1::2])]
    return values[0]


def exchange_sum(value, axis):
    return tree_sum(from_all(value, axis))


def exchange_rows(value, axis):
    values = from_all(value, axis)
    me = lax.axis_index(axis)
    whole = jnp.zeros((len(values),) + value.shape, value.dtype)
    for distance, piece in enumerate(values):
        whole = lax.dynamic_update_index_in_dim(whole, piece, me ^ distance, 0)
    return whole


def body(
    tokens,
    segment_ids,
    first_gain,
    first_shift,
    second_gain,
    second_shift,
    qkv_weight,
    qkv_bias,
    out_weight,
    out_bias,
    up_projection_weight,
    up_bias,
    down_weight,
    down_bias,
    cotangent,
):
    rows, width = tokens.shape
    qkv_cols = 3 * HD
    segment = segment_ids[0]
    group_rows = segment.shape[0]
    ring = Ring("tensor")
    far = ring.far
    half = rows // 2
    shard_rows = qkv_weight.shape[0]
    dp_start = lax.axis_index("dp") * shard_rows

    x_values = tokens.astype(F32)
    normed, inv_std = normalize(x_values)
    normed_low = normed.astype(BF16)
    up1, down1 = ring.up(normed_low), ring.down(normed_low)

    qkv_weight, up_projection_weight, first_gain, second_gain, first_shift, second_shift = after(
        (qkv_weight, up_projection_weight, first_gain, second_gain, first_shift, second_shift),
        normed_low,
    )
    w_qkv = qkv_weight.reshape(shard_rows, qkv_cols).astype(F32)
    w_up = up_projection_weight.astype(F32)

    def shard(vector):
        return lax.dynamic_slice(vector, (dp_start,), (shard_rows,)).astype(F32)

    gain1, gain2 = shard(first_gain), shard(second_gain)
    shift1, shift2 = shard(first_shift), shard(second_shift)
    scaled = jnp.concatenate(
        [w_qkv * gain1[:, None], w_up * gain2[:, None]], axis=1
    ).astype(BF16)
    w_in = lax.all_gather(scaled, "dp", axis=0, tiled=True)
    def row_of(offset):
        return ring.slot(offset) * rows

    def pair(step):
        return row_of(-step)

    w_out = after(jnp.concatenate([out_weight.T, down_weight.T], axis=1), scaled)
    shift_part = jnp.concatenate(
        [jnp.sum(w_qkv * shift1[:, None], axis=0), jnp.sum(w_up * shift2[:, None], axis=0)]
    )
    up1, down1, w_out, shift_part, slots = tie(up1, down1, w_out, shift_part, ring.slots)
    up2, down2 = ring.up(up1), ring.down(down1)
    w_back = lax.all_gather(w_out, "dp", axis=0, tiled=True)
    in_bias = exchange_sum(shift_part[None], "dp") + jnp.concatenate(
        [qkv_bias.reshape(-1), up_bias]
    ).astype(F32)[None]
    start = segment_starts(after(segment, up1))
    cosine, sine = rotation_tables(jnp.arange(group_rows, dtype=jnp.int32) - start)
    block_at = jnp.arange(group_rows // rows, dtype=jnp.int32)
    reach = jnp.clip(block_at - start[::rows] // rows + 1, 1, LONGEST // rows + 1)
    start = start[:, None]
    up2, down2, cosine, sine, start, in_bias, slots, reach = tie(
        up2, down2, cosine, sine, start, in_bias, slots, reach
    )

    up3, down3 = ring.up(up2), ring.down(down2)
    bufs = project([after(normed_low, up2), up1, down1], 0, w_in, in_bias, group_rows, None)
    up3, down3, *bufs = tie(up3, down3, *bufs)

    far_up, far_down = ring.up(up3[:half]), ring.down(down3[half:])
    cot_own = after(cotangent, up3, down3)
    cot_up1, cot_down1 = ring.up(cot_own), ring.down(cot_own)
    bufs = project([up2, down2, up3, down3], pair(2), w_in, in_bias, group_rows, bufs)
    far_up, far_down, cot_up1, cot_down1, *bufs = tie(far_up, far_down, cot_up1, cot_down1, *bufs)

    cot_up2, cot_down2 = ring.up(cot_up1), ring.down(cot_down1)
    bufs = project([far_up, far_down], row_of(far), w_in, in_bias, group_rows, bufs)
    proj, mixed, slope, normed_all = bufs
    mixed, query, keys, values, lse = attend(slots, reach, proj, cosine, sine, start, mixed, rows)
    cot_up2, cot_down2, mixed, slope = tie(cot_up2, cot_down2, mixed, slope)

    def split(block):
        return block[:half], block[half:]

    def send(pair_of_rows):
        return ring.up(pair_of_rows[0]), ring.down(pair_of_rows[1])

    def add(parts, step, moving):
        moving = [value.astype(F32) for value in moving]
        if step == 1:
            moving = [
                jnp.pad(moving[0], ((0, rows - half), (0, 0))),
                jnp.pad(moving[1], ((half, 0), (0, 0))),
            ]
        at = [row_of(far - step), row_of(step - far)]
        return tuple(
            (parts[first - rows : first].astype(F32) + value).astype(BF16)
            for first, value in zip(at, moving)
        )

    def out_part(first, count):
        return nt_dot(mixed[first : first + count], w_back)

    def grad_part(first, count):
        return nt_dot(d_in[first : first + count], w_in)

    rest = group_rows - 2 * rows

    cot_up3, cot_down3 = ring.up(cot_up2), ring.down(cot_down2)
    out_far = split(out_part(row_of(far), rows).astype(BF16))
    grads = back([cot_own, cot_up1, cot_down1, cot_up2, cot_down2], 0, w_back, slope, None)
    cot_up3, cot_down3, mixed, out_far, *grads = tie(cot_up3, cot_down3, mixed, out_far, *grads)

    cot_far_up, cot_far_down = ring.up(cot_up3[:half]), ring.down(cot_down3[half:])
    moving = send(out_far)
    out_rest = out_part(rows, rest).astype(BF16)
    grads = back([cot_up3, cot_down3], pair(3), w_back, slope, grads)
    cot_far_up, cot_far_down, moving, out_rest, grads, mixed = tie(
        cot_far_up, cot_far_down, moving, out_rest, tuple(grads), mixed
    )

    moving = send(add(out_rest, 1, moving))
    d_attn, d_in, cot_all = back([cot_far_up, cot_far_down], row_of(far), w_back, slope, grads)
    d_in = attend_back(
        slots, reach, d_attn, query, keys, values, lse, start, cosine, sine, d_in, rows
    )
    moving, out_rest, d_in, cot_all, mixed = tie(moving, out_rest, d_in, cot_all, mixed)

    moving = send(add(out_rest, 2, moving))
    grad_far = split(grad_part(row_of(far), rows).astype(BF16))
    raw_in = tn_dot(normed_all, d_in).astype(BF16)
    moving, out_rest, grad_far, raw_in, d_in, cot_all, mixed = tie(
        moving, out_rest, grad_far, raw_in, d_in, cot_all, mixed
    )

    raw_in = lax.psum_scatter(raw_in, "dp", scatter_dimension=0, tiled=True)
    added = add(out_rest, 3, moving)
    *added, d_in = tie(*added, d_in)
    moving = send(added)
    grad_moving = send(grad_far)
    grad_rest = grad_part(rows, rest).astype(BF16)
    in_sum = jnp.sum(d_in, axis=0, dtype=F32)[None]
    moving, grad_moving, grad_rest, in_sum, mixed, cot_all, d_in = tie(
        moving, grad_moving, grad_rest, in_sum, mixed, cot_all, d_in
    )

    added = add(grad_rest, 1, grad_moving)
    *added, mixed, cot_all, moving, d_in, in_sum = tie(*added, mixed, cot_all, moving, d_in, in_sum)
    grad_moving = send(added)
    out_grad = tn_dot(mixed, cot_all).astype(BF16)
    summed = out_part(0, rows) + moving[0].astype(F32) + moving[1].astype(F32)
    output = (x_values + out_bias.astype(F32) + down_bias.astype(F32) + summed).astype(BF16)
    in_sum = exchange_sum(in_sum, "dp")
    grad_moving, in_sum, output, out_grad, d_in = tie(
        grad_moving, in_sum, output, out_grad, d_in
    )
    out_grad = lax.psum_scatter(
        after(out_grad, raw_in), "dp", scatter_dimension=1, tiled=True
    )

    added = add(grad_rest, 2, grad_moving)
    *added, in_sum, d_in = tie(*added, in_sum, d_in)
    grad_moving = send(added)
    qkv_sum, up_sum = in_sum[:, :qkv_cols], in_sum[:, qkv_cols:]
    raw_qkv, raw_up = raw_in[:, :qkv_cols].astype(F32), raw_in[:, qkv_cols:].astype(F32)
    cot_values = cotangent.astype(F32)
    stats = jnp.stack(
        [
            jnp.sum(w_qkv * raw_qkv, axis=1),
            jnp.sum(w_qkv * qkv_sum, axis=1),
            jnp.sum(w_up * raw_up, axis=1),
            jnp.sum(w_up * up_sum, axis=1),
        ]
    )
    bias_part = jnp.sum(cot_values, axis=0).reshape(4, -1)
    stats = exchange_rows(jnp.concatenate([stats, bias_part], axis=1), "dp")
    bias_part = jnp.sum(stats[:, :, shard_rows:], axis=0).reshape(1, width)
    stats = jnp.transpose(stats[:, :, :shard_rows], (1, 0, 2)).reshape(4, width)
    stats = jnp.concatenate([stats, bias_part], axis=0)
    stats = stats + swap(stats, "tensor", 1)
    grad_last = grad_part(0, rows)
    grad_moving, stats, raw_in, grad_last = tie(grad_moving, stats, raw_in, grad_last)

    added = add(grad_rest, 3, grad_moving)
    *added, raw_in, stats = tie(*added, raw_in, stats)
    grad_moving = send(added)
    distances = range(2, ring.size, 2)
    stats = tree_sum([stats] + [swap(stats, "tensor", step) for step in distances])
    raw_qkv, raw_up = raw_in[:, :qkv_cols].astype(F32), raw_in[:, qkv_cols:].astype(F32)
    qkv_weight_grad = raw_qkv * gain1[:, None] + shift1[:, None] * qkv_sum
    up_weight_grad = raw_up * gain2[:, None] + shift2[:, None] * up_sum
    out_grad = out_grad.astype(F32)
    out_weight_grad, down_weight_grad = out_grad[:HD], out_grad[HD:]
    grad_moving, out_weight_grad, down_weight_grad = tie(
        grad_moving, out_weight_grad, down_weight_grad
    )
    grad_normed = grad_last + grad_moving[0].astype(F32) + grad_moving[1].astype(F32)
    layer_input_gradient = cot_values + inv_std * (
        grad_normed
        - jnp.mean(grad_normed, axis=1, keepdims=True)
        - normed * jnp.mean(grad_normed * normed, axis=1, keepdims=True)
    )
    return (
        output,
        layer_input_gradient,
        stats[0],
        stats[1],
        stats[2],
        stats[3],
        qkv_weight_grad.reshape(shard_rows, 1, qkv_cols),
        qkv_sum,
        out_weight_grad,
        stats[4],
        up_weight_grad,
        up_sum[0],
        down_weight_grad,
        stats[4],
    )


def solution(mesh):
    return jax.shard_map(
        body,
        mesh=mesh,
        in_specs=(
            P(("dp", "tensor"), None),
            P("dp", None),
            P(),
            P(),
            P(),
            P(),
            P("dp", "tensor", None),
            P("tensor", None),
            P("tensor", "dp"),
            P(),
            P("dp", "tensor"),
            P("tensor"),
            P("tensor", "dp"),
            P(),
            P(("dp", "tensor"), None),
        ),
        out_specs=(
            P(("dp", "tensor"), None),
            P(("dp", "tensor"), None),
            P(),
            P(),
            P(),
            P(),
            P("dp", "tensor", None),
            P("tensor", None),
            P("tensor", "dp"),
            P(),
            P("dp", "tensor"),
            P("tensor"),
            P("tensor", "dp"),
            P(),
        ),
        check_vma=False,
    )
```

```python
import functools
import math

import jax
import jax.numpy as jnp
from jax import lax
from jax.experimental import pallas as pl
from jax.experimental.pallas import tpu as pltpu
from jax.sharding import PartitionSpec as P

HD = 256
ROT = 64
LONGEST = 1024

NORM_EPS = 1e-05
MASK_FILL = -1e30
F32 = jnp.float32
BF16 = jnp.bfloat16
TILE = 256
MIB = 1024 * 1024
PROJECT_MIB = 36
BACK_MIB = 36
ATTEND_MIB = 28
ATTEND_BACK_MIB = 40


def normalize(values):
    mean_val = jnp.mean(values, axis=-1, keepdims=True)
    centred = values - mean_val
    spread = jnp.mean(centred * centred, axis=-1, keepdims=True)
    inv_std = lax.rsqrt(spread + NORM_EPS)
    return (centred * inv_std, inv_std)


def segment_starts(segment):
    row_count = segment.shape[0]
    position_index = jnp.arange(row_count, dtype=jnp.int32)
    starts = jnp.concatenate([jnp.ones((1,), dtype=jnp.bool_), segment[1:] != segment[:-1]])
    return lax.cummax(jnp.where(starts, position_index, jnp.zeros_like(position_index)), axis=0)


def rotation_tables(position):
    half_dims = ROT // 2
    lane = jnp.arange(128, dtype=jnp.int32)
    inv_freq = 10000.0 ** (-2.0 * (lane % half_dims).astype(F32) / ROT)
    angles = position.astype(F32)[:, None] * inv_freq[None, :]
    turned = (lane < ROT)[None, :]
    sign = jnp.where(lane < half_dims, -1.0, 1.0).astype(F32)[None, :]
    cosine = jnp.where(turned, jnp.cos(angles), 1.0)
    sine = jnp.where(turned, sign * jnp.sin(angles), 0.0)
    return cosine, sine


def turn(values, cosine, sine):
    head = values[:, :128]
    lane = lax.broadcasted_iota(jnp.int32, head.shape, 1)
    partner = jnp.where(
        lane < ROT // 2, pltpu.roll(head, 128 - ROT // 2, 1), pltpu.roll(head, ROT // 2, 1)
    )
    return jnp.concatenate([head * cosine + partner * sine, values[:, 128:]], axis=1)


def tie(*values):
    return lax.optimization_barrier(values)


def after(value, *others):
    return lax.optimization_barrier((value, others))[0]


def nt_dot(a, b):
    return lax.dot_general(a, b, (((1,), (1,)), ((), ())), preferred_element_type=F32)


def tn_dot(a, b):
    return lax.dot_general(a, b, (((0,), (0,)), ((), ())), preferred_element_type=F32)


def params(mib):
    return pltpu.CompilerParams(dimension_semantics=("arbitrary",), vmem_limit_bytes=mib * MIB)


def in_hbm(*values):
    return [pltpu.with_memory_space_constraint(value, pltpu.HBM) for value in values]


def fill(ins, rows_ref):
    at = 0
    for ref in ins:
        rows_ref[at : at + ref.shape[0], :] = ref[...]
        at += ref.shape[0]


def project_kernel(pieces, qkv_tiles, refs):
    w_ref, bias_ref = refs[pieces], refs[pieces + 1]
    proj_ref, mixed_ref, slope_ref, rows_ref = refs[-4:]
    j = pl.program_id(0)

    @pl.when(j == 0)
    def _():
        fill(refs[:pieces], rows_ref)

    def product():
        return jnp.dot(rows_ref[...], w_ref[...], preferred_element_type=F32) + bias_ref[...]

    @pl.when(j < qkv_tiles)
    def _():
        proj_ref[...] = product()

    @pl.when(j >= qkv_tiles)
    def _():
        out = product()
        cdf = 0.5 * (1.0 + lax.erf(out * (1.0 / math.sqrt(2.0))))
        mixed_ref[...] = (out * cdf).astype(BF16)
        density = jnp.exp(-0.5 * out * out) * (1.0 / math.sqrt(2.0 * math.pi))
        slope_ref[...] = (cdf + out * density).astype(BF16)


def aligned(col):
    return pl.multiple_of(col, TILE)


def at_element(rows, cols, index):
    return pl.BlockSpec((pl.Element(rows), pl.Element(cols)), index)


def in_place(kernel, grid, pieces, row, extra, extra_specs, bufs, buf_types, out_specs, mib, cost, name):
    given = () if bufs is None else tuple(bufs)
    first = len(pieces) + len(extra)
    return pl.pallas_call(
        lambda *refs: kernel(refs),
        grid=grid,
        in_specs=[pl.BlockSpec(piece.shape, lambda j: (0, 0)) for piece in pieces]
        + extra_specs
        + [pl.BlockSpec(memory_space=pltpu.HBM)] * len(given),
        out_specs=out_specs,
        out_shape=[pltpu.HBM(shape, dtype) for shape, dtype in buf_types],
        input_output_aliases={first + i: i for i in range(len(given))},
        compiler_params=params(mib),
        cost_estimate=cost,
        name=name,
    )(*in_hbm(*pieces, *extra), *given)


def project(pieces, row, weight, bias, group_rows, bufs):
    width, cols = weight.shape
    count = sum(piece.shape[0] for piece in pieces)
    qkv_tiles = 3 * HD // TILE
    hidden = cols - 3 * HD
    up_tile = lambda j: jnp.maximum(j - qkv_tiles, 0) * TILE
    return in_place(
        functools.partial(project_kernel, len(pieces), qkv_tiles),
        (cols // TILE,),
        pieces,
        row,
        (weight, bias),
        [
            pl.BlockSpec((width, TILE), lambda j: (0, j)),
            pl.BlockSpec((1, TILE), lambda j: (0, j)),
        ],
        bufs,
        [
            ((group_rows, 3 * HD), F32),
            ((group_rows, HD + hidden), BF16),
            ((group_rows, hidden), BF16),
            ((group_rows, width), BF16),
        ],
        [
            at_element(count, TILE, lambda j: (row, aligned(jnp.minimum(j, qkv_tiles - 1) * TILE))),
            at_element(count, TILE, lambda j: (row, aligned(HD + up_tile(j)))),
            at_element(count, TILE, lambda j: (row, aligned(up_tile(j)))),
            at_element(count, width, lambda j: (row, 0)),
        ],
        PROJECT_MIB,
        pl.CostEstimate(
            flops=2 * count * width * cols,
            bytes_accessed=2 * (width * cols + 2 * count * width) + 8 * count * cols // 2,
            transcendentals=2 * count * hidden,
        ),
        "project",
    )


def back_kernel(pieces, refs):
    w_ref, slope_ref = refs[pieces], refs[pieces + 1]
    attn_ref, d_in_ref, rows_ref = refs[-3:]
    j = pl.program_id(0)

    @pl.when(j == 0)
    def _():
        fill(refs[:pieces], rows_ref)

    out = jnp.dot(rows_ref[...], w_ref[...], preferred_element_type=F32)

    @pl.when(j == 0)
    def _():
        attn_ref[...] = out.astype(BF16)

    @pl.when(j > 0)
    def _():
        d_in_ref[...] = (out * slope_ref[...].astype(F32)).astype(BF16)


def back(pieces, row, weight, slope, bufs):
    width, cols = weight.shape
    group_rows, hidden = slope.shape
    count = sum(piece.shape[0] for piece in pieces)
    up_tile = lambda j: jnp.maximum(j - 1, 0) * TILE
    return in_place(
        functools.partial(back_kernel, len(pieces)),
        (cols // TILE,),
        pieces,
        row,
        (weight, slope),
        [
            pl.BlockSpec((width, TILE), lambda j: (0, j)),
            at_element(count, TILE, lambda j: (row, aligned(up_tile(j)))),
        ],
        bufs,
        [
            ((group_rows, HD), BF16),
            ((group_rows, 3 * HD + hidden), BF16),
            ((group_rows, width), BF16),
        ],
        [
            at_element(count, HD, lambda j: (row, 0)),
            at_element(count, TILE, lambda j: (row, aligned(3 * HD + up_tile(j)))),
            at_element(count, width, lambda j: (row, 0)),
        ],
        BACK_MIB,
        pl.CostEstimate(
            flops=2 * count * width * cols,
            bytes_accessed=2 * (width * cols + 2 * count * width + 3 * count * cols),
            transcendentals=0,
        ),
        "back",
    )


def window_mask(block, rows, count, start_ref):
    shape = (rows, count * rows)
    key_at = (block - count + 1) * rows + lax.broadcasted_iota(jnp.int32, shape, 1)
    query_at = block * rows + lax.broadcasted_iota(jnp.int32, shape, 0)
    return (key_at >= start_ref[...]) & (key_at <= query_at)


def by_count(reach_ref, rows, visit):
    block = pl.program_id(0)
    for count in range(1, LONGEST // rows + 2):

        @pl.when(reach_ref[block] == count)
        def _():
            first = pl.multiple_of((block - count + 1) * rows, rows)
            visit(count, pl.ds(first, count * rows))


def attend_kernel(
    rows, slot_ref, reach_ref, proj_ref, cos_ref, sin_ref, start_ref, _,
    mixed_ref, q_ref, k_ref, v_ref, lse_ref,
):
    block = pl.program_id(0)
    cosine, sine = cos_ref[...], sin_ref[...]
    here = pl.ds(pl.multiple_of(block * rows, rows), rows)
    q_ref[...] = turn(proj_ref[:, :HD], cosine, sine).astype(BF16)
    k_ref[here, :] = turn(proj_ref[:, HD : 2 * HD], cosine, sine).astype(BF16)
    v_ref[here, :] = proj_ref[:, 2 * HD :].astype(BF16)

    def visit(count, window):
        scores = nt_dot(q_ref[...], k_ref[window, :]) * (1.0 / math.sqrt(HD))
        scores = jnp.where(window_mask(block, rows, count, start_ref), scores, MASK_FILL)
        top = jnp.max(scores, axis=1, keepdims=True)
        weights = jnp.exp(scores - top)
        total = jnp.sum(weights, axis=1, keepdims=True)
        low = (weights * (1.0 / total)).astype(BF16)
        mixed_ref[...] = jnp.dot(low, v_ref[window, :], preferred_element_type=F32).astype(BF16)
        lse_ref[...] = top + jnp.log(total)

    by_count(reach_ref, rows, visit)


def attend(slots, reach, proj, cosine, sine, start, mixed, rows):
    group_rows = proj.shape[0]
    by_slot = lambda i, slot, reach: (slot[i], 0)
    in_order = lambda i, slot, reach: (i, 0)
    whole = lambda i, slot, reach: (0, 0)
    return pl.pallas_call(
        functools.partial(attend_kernel, rows),
        grid_spec=pltpu.PrefetchScalarGridSpec(
            num_scalar_prefetch=2,
            grid=(group_rows // rows,),
            in_specs=[
                pl.BlockSpec((rows, 3 * HD), by_slot),
                pl.BlockSpec((rows, 128), in_order),
                pl.BlockSpec((rows, 128), in_order),
                pl.BlockSpec((rows, 1), in_order),
                pl.BlockSpec(memory_space=pltpu.HBM),
            ],
            out_specs=[
                pl.BlockSpec((rows, HD), by_slot),
                pl.BlockSpec((rows, HD), in_order),
                pl.BlockSpec((group_rows, HD), whole),
                pl.BlockSpec((group_rows, HD), whole),
                pl.BlockSpec((rows, 1), in_order),
            ],
        ),
        out_shape=[
            pltpu.HBM(mixed.shape, BF16),
            pltpu.HBM((group_rows, HD), BF16),
            pltpu.HBM((group_rows, HD), BF16),
            pltpu.HBM((group_rows, HD), BF16),
            pltpu.HBM((group_rows, 1), F32),
        ],
        input_output_aliases={6: 0},
        compiler_params=params(ATTEND_MIB),
        cost_estimate=pl.CostEstimate(
            flops=4 * group_rows * LONGEST * HD,
            bytes_accessed=group_rows * HD * 22,
            transcendentals=group_rows * LONGEST,
        ),
        name="attend",
    )(slots, reach, *in_hbm(proj, cosine, sine, start), mixed)


def attend_back_kernel(
    rows, slot_ref, reach_ref, d_attn_ref, q_ref, k_ref, v_ref, lse_ref, start_ref, cos_ref, sin_ref,
    _, d_proj_ref, dk_ref, dv_ref,
):
    block = pl.program_id(0)
    blocks = pl.num_programs(0)
    scale = 1.0 / math.sqrt(HD)
    here = pl.ds(pl.multiple_of(block * rows, rows), rows)
    slot = pl.ds(pl.multiple_of(slot_ref[block] * rows, rows), rows)
    dk_ref[here, :] = jnp.zeros((rows, HD), F32)
    dv_ref[here, :] = jnp.zeros((rows, HD), F32)

    def visit(count, window):
        query, d_attn, keys = q_ref[...], d_attn_ref[...], k_ref[window, :]
        scores = nt_dot(query, keys) * scale
        mask = window_mask(block, rows, count, start_ref)
        probs = jnp.exp(jnp.where(mask, scores - lse_ref[...], MASK_FILL))
        d_probs = nt_dot(d_attn, v_ref[window, :])
        inner = jnp.sum(probs * d_probs, axis=1, keepdims=True)
        d_scores = (probs * (d_probs - inner)).astype(BF16)
        d_query = jnp.dot(d_scores, keys, preferred_element_type=F32) * scale
        dk_ref[window, :] += tn_dot(d_scores, query)
        dv_ref[window, :] += tn_dot(probs.astype(BF16), d_attn)
        d_proj_ref[slot, :HD] = turn(d_query, cos_ref[here, :], -sin_ref[here, :]).astype(BF16)

    by_count(reach_ref, rows, visit)

    @pl.when(block == blocks - 1)
    def _():
        def finish(i, carry):
            own = pl.ds(pl.multiple_of(i * rows, rows), rows)
            to = pl.ds(pl.multiple_of(slot_ref[i] * rows, rows), rows)
            d_key = turn(dk_ref[own, :] * scale, cos_ref[own, :], -sin_ref[own, :])
            d_proj_ref[to, HD : 2 * HD] = d_key.astype(BF16)
            d_proj_ref[to, 2 * HD :] = dv_ref[own, :].astype(BF16)
            return carry

        lax.fori_loop(0, blocks, finish, 0)


def attend_back(slots, reach, d_attn, query, keys, values, lse, start, cosine, sine, d_in, rows):
    group_rows = query.shape[0]
    by_slot = lambda i, slot, reach: (slot[i], 0)
    in_order = lambda i, slot, reach: (i, 0)
    whole = lambda i, slot, reach: (0, 0)
    return pl.pallas_call(
        functools.partial(attend_back_kernel, rows),
        grid_spec=pltpu.PrefetchScalarGridSpec(
            num_scalar_prefetch=2,
            grid=(group_rows // rows,),
            in_specs=[
                pl.BlockSpec((rows, HD), by_slot),
                pl.BlockSpec((rows, HD), in_order),
                pl.BlockSpec((group_rows, HD), whole),
                pl.BlockSpec((group_rows, HD), whole),
                pl.BlockSpec((rows, 1), in_order),
                pl.BlockSpec((rows, 1), in_order),
                pl.BlockSpec((group_rows, 128), whole),
                pl.BlockSpec((group_rows, 128), whole),
                pl.BlockSpec(memory_space=pltpu.HBM),
            ],
            out_specs=pl.BlockSpec((group_rows, 3 * HD), whole),
            scratch_shapes=[pltpu.VMEM((group_rows, HD), F32), pltpu.VMEM((group_rows, HD), F32)],
        ),
        out_shape=pltpu.HBM(d_in.shape, BF16),
        input_output_aliases={10: 0},
        compiler_params=params(ATTEND_BACK_MIB),
        cost_estimate=pl.CostEstimate(
            flops=10 * group_rows * LONGEST * HD,
            bytes_accessed=group_rows * HD * 20,
            transcendentals=group_rows * LONGEST,
        ),
        name="attend_back",
    )(slots, reach, *in_hbm(d_attn, query, keys, values, lse, start, cosine, sine), d_in)


class Ring:
    def __init__(self, axis):
        self.axis = axis
        size = lax.axis_size(axis)
        order = list(range(0, size, 2)) + list(range(size - 1, 0, -2))
        place = [order.index(i) for i in range(size)]
        self.size, self.far = size, size // 2
        self.up_pairs = [(order[i], order[(i + 1) % size]) for i in range(size)]
        self.down_pairs = [(order[i], order[(i - 1) % size]) for i in range(size)]
        slot_of = [0] * size
        for offset in range(size):
            slot_of[offset] = self.slot(offset)
        here = jnp.array(place, jnp.int32)[lax.axis_index(axis)]
        offsets = (jnp.array(place, jnp.int32) - here + size) % size
        self.slots = jnp.array(slot_of, jnp.int32)[offsets]

    def slot(self, offset):
        offset %= self.size
        if offset == 0:
            return 0
        if offset == self.far:
            return self.size - 1
        return 2 * offset if offset < self.far else 2 * (self.size - offset) - 1

    def up(self, value):
        return lax.ppermute(value, self.axis, self.up_pairs)

    def down(self, value):
        return lax.ppermute(value, self.axis, self.down_pairs)


def swap(value, axis, step):
    return lax.ppermute(value, axis, [(i, i ^ step) for i in range(lax.axis_size(axis))])


def from_all(value, axis):
    return [value] + [swap(value, axis, step) for step in range(1, lax.axis_size(axis))]


def tree_sum(values):
    while len(values) > 1:
        values = [a + b for a, b in zip(values[0::2], values[1::2])]
    return values[0]


def exchange_sum(value, axis):
    return tree_sum(from_all(value, axis))


def exchange_rows(value, axis):
    values = from_all(value, axis)
    me = lax.axis_index(axis)
    whole = jnp.zeros((len(values),) + value.shape, value.dtype)
    for distance, piece in enumerate(values):
        whole = lax.dynamic_update_index_in_dim(whole, piece, me ^ distance, 0)
    return whole


def body(
    tokens,
    segment_ids,
    first_gain,
    first_shift,
    second_gain,
    second_shift,
    qkv_weight,
    qkv_bias,
    out_weight,
    out_bias,
    up_projection_weight,
    up_bias,
    down_weight,
    down_bias,
    cotangent,
):
    rows, width = tokens.shape
    qkv_cols = 3 * HD
    segment = segment_ids[0]
    group_rows = segment.shape[0]
    ring = Ring("tensor")
    far = ring.far
    half = rows // 2
    shard_rows = qkv_weight.shape[0]
    dp_start = lax.axis_index("dp") * shard_rows

    x_values = tokens.astype(F32)
    normed, inv_std = normalize(x_values)
    normed_low = normed.astype(BF16)
    up1, down1 = ring.up(normed_low), ring.down(normed_low)

    w_qkv = qkv_weight.reshape(shard_rows, qkv_cols).astype(F32)
    w_up = up_projection_weight.astype(F32)

    def shard(vector):
        return lax.dynamic_slice(vector, (dp_start,), (shard_rows,)).astype(F32)

    gain1, gain2 = shard(first_gain), shard(second_gain)
    shift1, shift2 = shard(first_shift), shard(second_shift)
    scaled = jnp.concatenate(
        [w_qkv * gain1[:, None], w_up * gain2[:, None]], axis=1
    ).astype(BF16)
    w_in = lax.all_gather(scaled, "dp", axis=0, tiled=True)
    def row_of(offset):
        return ring.slot(offset) * rows

    def pair(step):
        return row_of(-step)

    w_out = after(jnp.concatenate([out_weight.T, down_weight.T], axis=1), scaled)
    shift_part = jnp.concatenate(
        [jnp.sum(w_qkv * shift1[:, None], axis=0), jnp.sum(w_up * shift2[:, None], axis=0)]
    )
    up1, down1, w_out, shift_part, slots = tie(up1, down1, w_out, shift_part, ring.slots)
    up2, down2 = ring.up(up1), ring.down(down1)
    w_back = lax.all_gather(w_out, "dp", axis=0, tiled=True)
    start = segment_starts(after(segment, up1))
    cosine, sine = rotation_tables(jnp.arange(group_rows, dtype=jnp.int32) - start)
    cosine, sine, shift_part = tie(cosine, sine, shift_part)
    in_bias = exchange_sum(shift_part[None], "dp") + jnp.concatenate(
        [qkv_bias.reshape(-1), up_bias]
    ).astype(F32)[None]
    block_at = jnp.arange(group_rows // rows, dtype=jnp.int32)
    reach = jnp.clip(block_at - start[::rows] // rows + 1, 1, LONGEST // rows + 1)
    start = start[:, None]
    up2, down2, cosine, sine, start, in_bias, slots, reach = tie(
        up2, down2, cosine, sine, start, in_bias, slots, reach
    )

    up3, down3 = ring.up(up2), ring.down(down2)
    bufs = project([after(normed_low, up2), up1, down1], 0, w_in, in_bias, group_rows, None)
    up3, down3, *bufs = tie(up3, down3, *bufs)

    far_up, far_down = ring.up(up3[:half]), ring.down(down3[half:])
    cot_own = after(cotangent, up3, down3)
    cot_up1, cot_down1 = ring.up(cot_own), ring.down(cot_own)
    bufs = project([up2, down2, up3, down3], pair(2), w_in, in_bias, group_rows, bufs)
    bias_part = jnp.sum(cot_own, axis=0, dtype=F32).reshape(4, -1)
    far_up, far_down, cot_up1, cot_down1, bias_part, *bufs = tie(
        far_up, far_down, cot_up1, cot_down1, bias_part, *bufs
    )

    cot_up2, cot_down2 = ring.up(cot_up1), ring.down(cot_down1)
    bufs = project([far_up, far_down], row_of(far), w_in, in_bias, group_rows, bufs)
    proj, mixed, slope, normed_all = bufs
    mixed, query, keys, values, lse = attend(slots, reach, proj, cosine, sine, start, mixed, rows)
    cot_up2, cot_down2, mixed, slope = tie(cot_up2, cot_down2, mixed, slope)

    def split(block):
        return block[:half], block[half:]

    def send(pair_of_rows):
        return ring.up(pair_of_rows[0]), ring.down(pair_of_rows[1])

    def add(parts, step, moving):
        moving = [value.astype(F32) for value in moving]
        if step == 1:
            moving = [
                jnp.pad(moving[0], ((0, rows - half), (0, 0))),
                jnp.pad(moving[1], ((half, 0), (0, 0))),
            ]
        at = [row_of(far - step), row_of(step - far)]
        return tuple(
            (parts[first - rows : first].astype(F32) + value).astype(BF16)
            for first, value in zip(at, moving)
        )

    def out_part(first, count):
        return nt_dot(mixed[first : first + count], w_back)

    def grad_part(first, count):
        return nt_dot(d_in[first : first + count], w_in)

    rest = group_rows - 2 * rows

    cot_up3, cot_down3 = ring.up(cot_up2), ring.down(cot_down2)
    out_far = split(out_part(row_of(far), rows).astype(BF16))
    grads = back([cot_own, cot_up1, cot_down1, cot_up2, cot_down2], 0, w_back, slope, None)
    cot_up3, cot_down3, mixed, out_far, *grads = tie(cot_up3, cot_down3, mixed, out_far, *grads)

    cot_far_up, cot_far_down = ring.up(cot_up3[:half]), ring.down(cot_down3[half:])
    moving = send(out_far)
    out_rest = out_part(rows, rest).astype(BF16)
    grads = back([cot_up3, cot_down3], pair(3), w_back, slope, grads)
    cot_far_up, cot_far_down, moving, out_rest, grads, mixed = tie(
        cot_far_up, cot_far_down, moving, out_rest, tuple(grads), mixed
    )

    moving = send(add(out_rest, 1, moving))
    d_attn, d_in, cot_all = back([cot_far_up, cot_far_down], row_of(far), w_back, slope, grads)
    d_in = attend_back(
        slots, reach, d_attn, query, keys, values, lse, start, cosine, sine, d_in, rows
    )
    moving, out_rest, d_in, cot_all, mixed = tie(moving, out_rest, d_in, cot_all, mixed)

    moving = send(add(out_rest, 2, moving))
    grad_far = split(grad_part(row_of(far), rows).astype(BF16))
    raw_in = tn_dot(normed_all, d_in).astype(BF16)
    moving, out_rest, grad_far, raw_in, d_in, cot_all, mixed = tie(
        moving, out_rest, grad_far, raw_in, d_in, cot_all, mixed
    )

    raw_in = lax.psum_scatter(raw_in, "dp", scatter_dimension=0, tiled=True)
    added = add(out_rest, 3, moving)
    *added, d_in = tie(*added, d_in)
    moving = send(added)
    grad_moving = send(grad_far)
    grad_rest = grad_part(rows, rest).astype(BF16)
    in_sum = jnp.sum(d_in, axis=0, dtype=F32)[None]
    moving, grad_moving, grad_rest, in_sum, mixed, cot_all, d_in = tie(
        moving, grad_moving, grad_rest, in_sum, mixed, cot_all, d_in
    )

    added = add(grad_rest, 1, grad_moving)
    *added, mixed, cot_all, moving, d_in, in_sum = tie(*added, mixed, cot_all, moving, d_in, in_sum)
    grad_moving = send(added)
    out_grad = tn_dot(mixed, cot_all).astype(BF16)
    summed = out_part(0, rows) + moving[0].astype(F32) + moving[1].astype(F32)
    output = (x_values + out_bias.astype(F32) + down_bias.astype(F32) + summed).astype(BF16)
    in_sum = exchange_sum(in_sum, "dp")
    grad_moving, in_sum, output, out_grad, d_in = tie(
        grad_moving, in_sum, output, out_grad, d_in
    )

    added = add(grad_rest, 2, grad_moving)
    out_grad = lax.psum_scatter(out_grad, "dp", scatter_dimension=1, tiled=True)
    *added, in_sum, d_in = tie(*added, in_sum, d_in)
    grad_moving = send(added)
    qkv_sum, up_sum = in_sum[:, :qkv_cols], in_sum[:, qkv_cols:]
    raw_qkv, raw_up = raw_in[:, :qkv_cols].astype(F32), raw_in[:, qkv_cols:].astype(F32)
    cot_values = cotangent.astype(F32)
    stats = jnp.stack(
        [
            jnp.sum(w_qkv * raw_qkv, axis=1),
            jnp.sum(w_qkv * qkv_sum, axis=1),
            jnp.sum(w_up * raw_up, axis=1),
            jnp.sum(w_up * up_sum, axis=1),
        ]
    )
    stats = exchange_rows(jnp.concatenate([stats, bias_part], axis=1), "dp")
    bias_part = jnp.sum(stats[:, :, shard_rows:], axis=0).reshape(1, width)
    stats = jnp.transpose(stats[:, :, :shard_rows], (1, 0, 2)).reshape(4, width)
    stats = jnp.concatenate([stats, bias_part], axis=0)
    stats = stats + swap(stats, "tensor", 1)
    grad_last = grad_part(0, rows)
    distances = range(2, ring.size, 2)
    others = [swap(stats, "tensor", step) for step in distances]
    grad_moving, stats, raw_in, grad_last = tie(grad_moving, stats, raw_in, grad_last)

    added = add(grad_rest, 3, grad_moving)
    *added, raw_in = tie(*added, raw_in)
    grad_moving = send(added)
    stats = tree_sum([stats] + others)
    raw_qkv, raw_up = raw_in[:, :qkv_cols].astype(F32), raw_in[:, qkv_cols:].astype(F32)
    qkv_weight_grad = raw_qkv * gain1[:, None] + shift1[:, None] * qkv_sum
    up_weight_grad = raw_up * gain2[:, None] + shift2[:, None] * up_sum
    stats, out_grad = tie(stats, out_grad)
    out_grad = out_grad.astype(F32)
    out_weight_grad, down_weight_grad = out_grad[:HD], out_grad[HD:]
    grad_moving, out_weight_grad, down_weight_grad = tie(
        grad_moving, out_weight_grad, down_weight_grad
    )
    grad_normed = grad_last + grad_moving[0].astype(F32) + grad_moving[1].astype(F32)
    layer_input_gradient = cot_values + inv_std * (
        grad_normed
        - jnp.mean(grad_normed, axis=1, keepdims=True)
        - normed * jnp.mean(grad_normed * normed, axis=1, keepdims=True)
    )
    return (
        output,
        layer_input_gradient,
        stats[0],
        stats[1],
        stats[2],
        stats[3],
        qkv_weight_grad.reshape(shard_rows, 1, qkv_cols),
        qkv_sum,
        out_weight_grad,
        stats[4],
        up_weight_grad,
        up_sum[0],
        down_weight_grad,
        stats[4],
    )


def solution(mesh):
    return jax.shard_map(
        body,
        mesh=mesh,
        in_specs=(
            P(("dp", "tensor"), None),
            P("dp", None),
            P(),
            P(),
            P(),
            P(),
            P("dp", "tensor", None),
            P("tensor", None),
            P("tensor", "dp"),
            P(),
            P("dp", "tensor"),
            P("tensor"),
            P("tensor", "dp"),
            P(),
            P(("dp", "tensor"), None),
        ),
        out_specs=(
            P(("dp", "tensor"), None),
            P(("dp", "tensor"), None),
            P(),
            P(),
            P(),
            P(),
            P("dp", "tensor", None),
            P("tensor", None),
            P("tensor", "dp"),
            P(),
            P("dp", "tensor"),
            P("tensor"),
            P("tensor", "dp"),
            P(),
        ),
        check_vma=False,
    )
```

```python
import functools
import math

import jax
import jax.numpy as jnp
from jax import lax
from jax.experimental import pallas as pl
from jax.experimental.pallas import tpu as pltpu
from jax.sharding import PartitionSpec as P

HD = 256
ROT = 64
LONGEST = 1024

NORM_EPS = 1e-05
MASK_FILL = -1e30
F32 = jnp.float32
BF16 = jnp.bfloat16
TILE = 256
MIB = 1024 * 1024
PROJECT_MIB = 36
BACK_MIB = 36
ATTEND_MIB = 28
ATTEND_BACK_MIB = 40


def normalize(values):
    mean_val = jnp.mean(values, axis=-1, keepdims=True)
    centred = values - mean_val
    spread = jnp.mean(centred * centred, axis=-1, keepdims=True)
    inv_std = lax.rsqrt(spread + NORM_EPS)
    return (centred * inv_std, inv_std)


def segment_starts(segment):
    row_count = segment.shape[0]
    position_index = jnp.arange(row_count, dtype=jnp.int32)
    starts = jnp.concatenate([jnp.ones((1,), dtype=jnp.bool_), segment[1:] != segment[:-1]])
    return lax.cummax(jnp.where(starts, position_index, jnp.zeros_like(position_index)), axis=0)


def rotation_tables(position):
    half_dims = ROT // 2
    lane = jnp.arange(128, dtype=jnp.int32)
    inv_freq = 10000.0 ** (-2.0 * (lane % half_dims).astype(F32) / ROT)
    angles = position.astype(F32)[:, None] * inv_freq[None, :]
    turned = (lane < ROT)[None, :]
    sign = jnp.where(lane < half_dims, -1.0, 1.0).astype(F32)[None, :]
    cosine = jnp.where(turned, jnp.cos(angles), 1.0)
    sine = jnp.where(turned, sign * jnp.sin(angles), 0.0)
    return cosine, sine


def turn(values, cosine, sine):
    head = values[:, :128]
    lane = lax.broadcasted_iota(jnp.int32, head.shape, 1)
    partner = jnp.where(
        lane < ROT // 2, pltpu.roll(head, 128 - ROT // 2, 1), pltpu.roll(head, ROT // 2, 1)
    )
    return jnp.concatenate([head * cosine + partner * sine, values[:, 128:]], axis=1)


def tie(*values):
    return lax.optimization_barrier(values)


def after(value, *others):
    return lax.optimization_barrier((value, others))[0]


def nt_dot(a, b):
    return lax.dot_general(a, b, (((1,), (1,)), ((), ())), preferred_element_type=F32)


def tn_dot(a, b):
    return lax.dot_general(a, b, (((0,), (0,)), ((), ())), preferred_element_type=F32)


def params(mib):
    return pltpu.CompilerParams(dimension_semantics=("arbitrary",), vmem_limit_bytes=mib * MIB)


def in_hbm(*values):
    return [pltpu.with_memory_space_constraint(value, pltpu.HBM) for value in values]


def fill(ins, rows_ref):
    at = 0
    for ref in ins:
        rows_ref[at : at + ref.shape[0], :] = ref[...]
        at += ref.shape[0]


def project_kernel(pieces, qkv_tiles, refs):
    w_ref, bias_ref = refs[pieces], refs[pieces + 1]
    proj_ref, mixed_ref, slope_ref, rows_ref = refs[-4:]
    j = pl.program_id(0)

    @pl.when(j == 0)
    def _():
        fill(refs[:pieces], rows_ref)

    def product():
        return jnp.dot(rows_ref[...], w_ref[...], preferred_element_type=F32) + bias_ref[...]

    @pl.when(j < qkv_tiles)
    def _():
        proj_ref[...] = product()

    @pl.when(j >= qkv_tiles)
    def _():
        out = product()
        cdf = 0.5 * (1.0 + lax.erf(out * (1.0 / math.sqrt(2.0))))
        mixed_ref[...] = (out * cdf).astype(BF16)
        density = jnp.exp(-0.5 * out * out) * (1.0 / math.sqrt(2.0 * math.pi))
        slope_ref[...] = (cdf + out * density).astype(BF16)


def aligned(col):
    return pl.multiple_of(col, TILE)


def at_element(rows, cols, index):
    return pl.BlockSpec((pl.Element(rows), pl.Element(cols)), index)


def in_place(kernel, grid, pieces, row, extra, extra_specs, bufs, buf_types, out_specs, mib, cost, name):
    given = () if bufs is None else tuple(bufs)
    first = len(pieces) + len(extra)
    return pl.pallas_call(
        lambda *refs: kernel(refs),
        grid=grid,
        in_specs=[pl.BlockSpec(piece.shape, lambda j: (0, 0)) for piece in pieces]
        + extra_specs
        + [pl.BlockSpec(memory_space=pltpu.HBM)] * len(given),
        out_specs=out_specs,
        out_shape=[pltpu.HBM(shape, dtype) for shape, dtype in buf_types],
        input_output_aliases={first + i: i for i in range(len(given))},
        compiler_params=params(mib),
        cost_estimate=cost,
        name=name,
    )(*in_hbm(*pieces, *extra), *given)


def project(pieces, row, weight, bias, group_rows, bufs):
    width, cols = weight.shape
    count = sum(piece.shape[0] for piece in pieces)
    qkv_tiles = 3 * HD // TILE
    hidden = cols - 3 * HD
    up_tile = lambda j: jnp.maximum(j - qkv_tiles, 0) * TILE
    return in_place(
        functools.partial(project_kernel, len(pieces), qkv_tiles),
        (cols // TILE,),
        pieces,
        row,
        (weight, bias),
        [
            pl.BlockSpec((width, TILE), lambda j: (0, j)),
            pl.BlockSpec((1, TILE), lambda j: (0, j)),
        ],
        bufs,
        [
            ((group_rows, 3 * HD), F32),
            ((group_rows, HD + hidden), BF16),
            ((group_rows, hidden), BF16),
            ((group_rows, width), BF16),
        ],
        [
            at_element(count, TILE, lambda j: (row, aligned(jnp.minimum(j, qkv_tiles - 1) * TILE))),
            at_element(count, TILE, lambda j: (row, aligned(HD + up_tile(j)))),
            at_element(count, TILE, lambda j: (row, aligned(up_tile(j)))),
            at_element(count, width, lambda j: (row, 0)),
        ],
        PROJECT_MIB,
        pl.CostEstimate(
            flops=2 * count * width * cols,
            bytes_accessed=2 * (width * cols + 2 * count * width) + 8 * count * cols // 2,
            transcendentals=2 * count * hidden,
        ),
        "project",
    )


def back_kernel(pieces, refs):
    w_ref, slope_ref = refs[pieces], refs[pieces + 1]
    attn_ref, d_in_ref, rows_ref = refs[-3:]
    j = pl.program_id(0)

    @pl.when(j == 0)
    def _():
        fill(refs[:pieces], rows_ref)

    out = jnp.dot(rows_ref[...], w_ref[...], preferred_element_type=F32)

    @pl.when(j == 0)
    def _():
        attn_ref[...] = out.astype(BF16)

    @pl.when(j > 0)
    def _():
        d_in_ref[...] = (out * slope_ref[...].astype(F32)).astype(BF16)


def back(pieces, row, weight, slope, bufs):
    width, cols = weight.shape
    group_rows, hidden = slope.shape
    count = sum(piece.shape[0] for piece in pieces)
    up_tile = lambda j: jnp.maximum(j - 1, 0) * TILE
    return in_place(
        functools.partial(back_kernel, len(pieces)),
        (cols // TILE,),
        pieces,
        row,
        (weight, slope),
        [
            pl.BlockSpec((width, TILE), lambda j: (0, j)),
            at_element(count, TILE, lambda j: (row, aligned(up_tile(j)))),
        ],
        bufs,
        [
            ((group_rows, HD), BF16),
            ((group_rows, 3 * HD + hidden), BF16),
            ((group_rows, width), BF16),
        ],
        [
            at_element(count, HD, lambda j: (row, 0)),
            at_element(count, TILE, lambda j: (row, aligned(3 * HD + up_tile(j)))),
            at_element(count, width, lambda j: (row, 0)),
        ],
        BACK_MIB,
        pl.CostEstimate(
            flops=2 * count * width * cols,
            bytes_accessed=2 * (width * cols + 2 * count * width + 3 * count * cols),
            transcendentals=0,
        ),
        "back",
    )


def window_mask(block, rows, count, start_ref):
    shape = (rows, count * rows)
    key_at = (block - count + 1) * rows + lax.broadcasted_iota(jnp.int32, shape, 1)
    query_at = block * rows + lax.broadcasted_iota(jnp.int32, shape, 0)
    return (key_at >= start_ref[:, :1]) & (key_at <= query_at)


def by_count(reach_ref, rows, visit):
    block = pl.program_id(0)
    for count in range(1, LONGEST // rows + 2):

        @pl.when(reach_ref[block] == count)
        def _():
            first = pl.multiple_of((block - count + 1) * rows, rows)
            visit(count, pl.ds(first, count * rows))


def attend_kernel(
    rows, slot_ref, reach_ref, proj_ref, cos_ref, sin_ref, start_ref, _,
    mixed_ref, q_ref, k_ref, v_ref, lse_ref,
):
    block = pl.program_id(0)
    cosine, sine = cos_ref[...], sin_ref[...]
    here = pl.ds(pl.multiple_of(block * rows, rows), rows)
    q_ref[...] = turn(proj_ref[:, :HD], cosine, sine).astype(BF16)
    k_ref[here, :] = turn(proj_ref[:, HD : 2 * HD], cosine, sine).astype(BF16)
    v_ref[here, :] = proj_ref[:, 2 * HD :].astype(BF16)

    def visit(count, window):
        scores = nt_dot(q_ref[...], k_ref[window, :]) * (1.0 / math.sqrt(HD))
        scores = jnp.where(window_mask(block, rows, count, start_ref), scores, MASK_FILL)
        top = jnp.max(scores, axis=1, keepdims=True)
        weights = jnp.exp(scores - top)
        total = jnp.sum(weights, axis=1, keepdims=True)
        low = (weights * (1.0 / total)).astype(BF16)
        mixed_ref[...] = jnp.dot(low, v_ref[window, :], preferred_element_type=F32).astype(BF16)
        lse_ref[...] = top + jnp.log(total)

    by_count(reach_ref, rows, visit)


def attend(slots, reach, proj, cosine, sine, start, mixed, rows):
    group_rows = proj.shape[0]
    by_slot = lambda i, slot, reach: (slot[i], 0)
    in_order = lambda i, slot, reach: (i, 0)
    whole = lambda i, slot, reach: (0, 0)
    return pl.pallas_call(
        functools.partial(attend_kernel, rows),
        grid_spec=pltpu.PrefetchScalarGridSpec(
            num_scalar_prefetch=2,
            grid=(group_rows // rows,),
            in_specs=[
                pl.BlockSpec((rows, 3 * HD), by_slot),
                pl.BlockSpec((rows, 128), in_order),
                pl.BlockSpec((rows, 128), in_order),
                pl.BlockSpec((rows, 128), in_order),
                pl.BlockSpec(memory_space=pltpu.HBM),
            ],
            out_specs=[
                pl.BlockSpec((rows, HD), by_slot),
                pl.BlockSpec((rows, HD), in_order),
                pl.BlockSpec((group_rows, HD), whole),
                pl.BlockSpec((group_rows, HD), whole),
                pl.BlockSpec((rows, 1), in_order),
            ],
        ),
        out_shape=[
            pltpu.HBM(mixed.shape, BF16),
            pltpu.HBM((group_rows, HD), BF16),
            pltpu.HBM((group_rows, HD), BF16),
            pltpu.HBM((group_rows, HD), BF16),
            pltpu.HBM((group_rows, 1), F32),
        ],
        input_output_aliases={6: 0},
        compiler_params=params(ATTEND_MIB),
        cost_estimate=pl.CostEstimate(
            flops=4 * group_rows * LONGEST * HD,
            bytes_accessed=group_rows * HD * 22,
            transcendentals=group_rows * LONGEST,
        ),
        name="attend",
    )(slots, reach, *in_hbm(proj, cosine, sine, start), mixed)


def attend_back_kernel(
    rows, slot_ref, reach_ref, d_attn_ref, q_ref, k_ref, v_ref, lse_ref, start_ref, cos_ref, sin_ref,
    _, d_proj_ref, dk_ref, dv_ref,
):
    block = pl.program_id(0)
    blocks = pl.num_programs(0)
    scale = 1.0 / math.sqrt(HD)
    here = pl.ds(pl.multiple_of(block * rows, rows), rows)
    slot = pl.ds(pl.multiple_of(slot_ref[block] * rows, rows), rows)
    dk_ref[here, :] = jnp.zeros((rows, HD), F32)
    dv_ref[here, :] = jnp.zeros((rows, HD), F32)

    def visit(count, window):
        query, d_attn, keys = q_ref[...], d_attn_ref[...], k_ref[window, :]
        scores = nt_dot(query, keys) * scale
        mask = window_mask(block, rows, count, start_ref)
        probs = jnp.exp(jnp.where(mask, scores - lse_ref[...], MASK_FILL))
        d_probs = nt_dot(d_attn, v_ref[window, :])
        inner = jnp.sum(probs * d_probs, axis=1, keepdims=True)
        d_scores = (probs * (d_probs - inner)).astype(BF16)
        d_query = jnp.dot(d_scores, keys, preferred_element_type=F32) * scale
        dk_ref[window, :] += tn_dot(d_scores, query)
        dv_ref[window, :] += tn_dot(probs.astype(BF16), d_attn)
        d_proj_ref[slot, :HD] = turn(d_query, cos_ref[here, :], -sin_ref[here, :]).astype(BF16)

    by_count(reach_ref, rows, visit)

    @pl.when(block == blocks - 1)
    def _():
        def finish(i, carry):
            own = pl.ds(pl.multiple_of(i * rows, rows), rows)
            to = pl.ds(pl.multiple_of(slot_ref[i] * rows, rows), rows)
            d_key = turn(dk_ref[own, :] * scale, cos_ref[own, :], -sin_ref[own, :])
            d_proj_ref[to, HD : 2 * HD] = d_key.astype(BF16)
            d_proj_ref[to, 2 * HD :] = dv_ref[own, :].astype(BF16)
            return carry

        lax.fori_loop(0, blocks, finish, 0)


def attend_back(slots, reach, d_attn, query, keys, values, lse, start, cosine, sine, d_in, rows):
    group_rows = query.shape[0]
    by_slot = lambda i, slot, reach: (slot[i], 0)
    in_order = lambda i, slot, reach: (i, 0)
    whole = lambda i, slot, reach: (0, 0)
    return pl.pallas_call(
        functools.partial(attend_back_kernel, rows),
        grid_spec=pltpu.PrefetchScalarGridSpec(
            num_scalar_prefetch=2,
            grid=(group_rows // rows,),
            in_specs=[
                pl.BlockSpec((rows, HD), by_slot),
                pl.BlockSpec((rows, HD), in_order),
                pl.BlockSpec((group_rows, HD), whole),
                pl.BlockSpec((group_rows, HD), whole),
                pl.BlockSpec((rows, 1), in_order),
                pl.BlockSpec((rows, 128), in_order),
                pl.BlockSpec((group_rows, 128), whole),
                pl.BlockSpec((group_rows, 128), whole),
                pl.BlockSpec(memory_space=pltpu.HBM),
            ],
            out_specs=pl.BlockSpec((group_rows, 3 * HD), whole),
            scratch_shapes=[pltpu.VMEM((group_rows, HD), F32), pltpu.VMEM((group_rows, HD), F32)],
        ),
        out_shape=pltpu.HBM(d_in.shape, BF16),
        input_output_aliases={10: 0},
        compiler_params=params(ATTEND_BACK_MIB),
        cost_estimate=pl.CostEstimate(
            flops=10 * group_rows * LONGEST * HD,
            bytes_accessed=group_rows * HD * 20,
            transcendentals=group_rows * LONGEST,
        ),
        name="attend_back",
    )(slots, reach, *in_hbm(d_attn, query, keys, values, lse, start, cosine, sine), d_in)


def finish_kernel(own_ref, up_ref, down_ref, tokens_ref, cot_ref, out_ref):
    normed, inv_std = normalize(tokens_ref[...].astype(F32))
    total = own_ref[...] + up_ref[...].astype(F32) + down_ref[...].astype(F32)
    out_ref[...] = cot_ref[...].astype(F32) + inv_std * (
        total
        - jnp.mean(total, axis=1, keepdims=True)
        - normed * jnp.mean(total * normed, axis=1, keepdims=True)
    )


def finish(own, up, down, tokens, cotangent):
    rows, width = tokens.shape
    step = rows // 2
    spec = pl.BlockSpec((step, width), lambda i: (i, 0))
    return pl.pallas_call(
        finish_kernel,
        grid=(rows // step,),
        in_specs=[spec] * 5,
        out_specs=spec,
        out_shape=jax.ShapeDtypeStruct((rows, width), F32),
        compiler_params=params(20),
        cost_estimate=pl.CostEstimate(
            flops=16 * rows * width, bytes_accessed=16 * rows * width, transcendentals=rows
        ),
        name="finish",
    )(own, up, down, tokens, cotangent)


class Ring:
    def __init__(self, axis):
        self.axis = axis
        size = lax.axis_size(axis)
        order = list(range(0, size, 2)) + list(range(size - 1, 0, -2))
        place = [order.index(i) for i in range(size)]
        self.size, self.far = size, size // 2
        self.up_pairs = [(order[i], order[(i + 1) % size]) for i in range(size)]
        self.down_pairs = [(order[i], order[(i - 1) % size]) for i in range(size)]
        slot_of = [0] * size
        for offset in range(size):
            slot_of[offset] = self.slot(offset)
        here = jnp.array(place, jnp.int32)[lax.axis_index(axis)]
        offsets = (jnp.array(place, jnp.int32) - here + size) % size
        self.slots = jnp.array(slot_of, jnp.int32)[offsets]

    def slot(self, offset):
        offset %= self.size
        if offset == 0:
            return 0
        if offset == self.far:
            return self.size - 1
        return 2 * offset if offset < self.far else 2 * (self.size - offset) - 1

    def up(self, value):
        return lax.ppermute(value, self.axis, self.up_pairs)

    def down(self, value):
        return lax.ppermute(value, self.axis, self.down_pairs)


def swap(value, axis, step):
    return lax.ppermute(value, axis, [(i, i ^ step) for i in range(lax.axis_size(axis))])


def from_all(value, axis):
    return [value] + [swap(value, axis, step) for step in range(1, lax.axis_size(axis))]


def tree_sum(values):
    while len(values) > 1:
        values = [a + b for a, b in zip(values[0::2], values[1::2])]
    return values[0]


def exchange_sum(value, axis):
    return tree_sum(from_all(value, axis))


def exchange_rows(value, axis):
    values = from_all(value, axis)
    me = lax.axis_index(axis)
    whole = jnp.zeros((len(values),) + value.shape, value.dtype)
    for distance, piece in enumerate(values):
        whole = lax.dynamic_update_index_in_dim(whole, piece, me ^ distance, 0)
    return whole


def body(
    tokens,
    segment_ids,
    first_gain,
    first_shift,
    second_gain,
    second_shift,
    qkv_weight,
    qkv_bias,
    out_weight,
    out_bias,
    up_projection_weight,
    up_bias,
    down_weight,
    down_bias,
    cotangent,
):
    rows, width = tokens.shape
    qkv_cols = 3 * HD
    segment = segment_ids[0]
    group_rows = segment.shape[0]
    ring = Ring("tensor")
    far = ring.far
    half = rows // 2
    shard_rows = qkv_weight.shape[0]
    dp_start = lax.axis_index("dp") * shard_rows

    x_values = tokens.astype(F32)
    normed, inv_std = normalize(x_values)
    normed_low = normed.astype(BF16)
    up1, down1 = ring.up(normed_low), ring.down(normed_low)

    w_qkv = qkv_weight.reshape(shard_rows, qkv_cols).astype(F32)
    w_up = up_projection_weight.astype(F32)

    def shard(vector):
        return lax.dynamic_slice(vector, (dp_start,), (shard_rows,)).astype(F32)

    gain1, gain2 = shard(first_gain), shard(second_gain)
    shift1, shift2 = shard(first_shift), shard(second_shift)
    scaled = jnp.concatenate(
        [w_qkv * gain1[:, None], w_up * gain2[:, None]], axis=1
    ).astype(BF16)
    w_in = lax.all_gather(scaled, "dp", axis=0, tiled=True)
    def row_of(offset):
        return ring.slot(offset) * rows

    def pair(step):
        return row_of(-step)

    w_out = after(jnp.concatenate([out_weight.T, down_weight.T], axis=1), scaled)
    shift_part = jnp.concatenate(
        [jnp.sum(w_qkv * shift1[:, None], axis=0), jnp.sum(w_up * shift2[:, None], axis=0)]
    )
    up1, down1, w_out, shift_part, slots = tie(up1, down1, w_out, shift_part, ring.slots)
    up2, down2 = ring.up(up1), ring.down(down1)
    w_back = lax.all_gather(w_out, "dp", axis=0, tiled=True)
    start = segment_starts(after(segment, up1))
    cosine, sine = rotation_tables(jnp.arange(group_rows, dtype=jnp.int32) - start)
    cosine, sine, shift_part = tie(cosine, sine, shift_part)
    in_bias = exchange_sum(shift_part[None], "dp") + jnp.concatenate(
        [qkv_bias.reshape(-1), up_bias]
    ).astype(F32)[None]
    block_at = jnp.arange(group_rows // rows, dtype=jnp.int32)
    reach = jnp.clip(block_at - start[::rows] // rows + 1, 1, LONGEST // rows + 1)
    start = jnp.broadcast_to(start[:, None], cosine.shape)
    up2, down2, cosine, sine, start, in_bias, slots, reach = tie(
        up2, down2, cosine, sine, start, in_bias, slots, reach
    )

    up3, down3 = ring.up(up2), ring.down(down2)
    bufs = project([after(normed_low, up2), up1, down1], 0, w_in, in_bias, group_rows, None)
    up3, down3, *bufs = tie(up3, down3, *bufs)

    far_up, far_down = ring.up(up3[:half]), ring.down(down3[half:])
    cot_own = after(cotangent, up3, down3)
    cot_up1, cot_down1 = ring.up(cot_own), ring.down(cot_own)
    bufs = project([up2, down2, up3, down3], pair(2), w_in, in_bias, group_rows, bufs)
    bias_part = jnp.sum(cot_own, axis=0, dtype=F32).reshape(4, -1)
    far_up, far_down, cot_up1, cot_down1, bias_part, *bufs = tie(
        far_up, far_down, cot_up1, cot_down1, bias_part, *bufs
    )

    cot_up2, cot_down2 = ring.up(cot_up1), ring.down(cot_down1)
    bufs = project([far_up, far_down], row_of(far), w_in, in_bias, group_rows, bufs)
    proj, mixed, slope, normed_all = bufs
    mixed, query, keys, values, lse = attend(slots, reach, proj, cosine, sine, start, mixed, rows)
    cot_up2, cot_down2, mixed, slope = tie(cot_up2, cot_down2, mixed, slope)

    def split(block):
        return block[:half], block[half:]

    def send(pair_of_rows):
        return ring.up(pair_of_rows[0]), ring.down(pair_of_rows[1])

    def add(parts, step, moving):
        moving = [value.astype(F32) for value in moving]
        if step == 1:
            moving = [
                jnp.pad(moving[0], ((0, rows - half), (0, 0))),
                jnp.pad(moving[1], ((half, 0), (0, 0))),
            ]
        at = [row_of(far - step), row_of(step - far)]
        return tuple(
            (parts[first - rows : first].astype(F32) + value).astype(BF16)
            for first, value in zip(at, moving)
        )

    def out_part(first, count):
        return nt_dot(mixed[first : first + count], w_back)

    def grad_part(first, count):
        return nt_dot(d_in[first : first + count], w_in)

    rest = group_rows - 2 * rows

    cot_up3, cot_down3 = ring.up(cot_up2), ring.down(cot_down2)
    out_far = split(out_part(row_of(far), rows).astype(BF16))
    grads = back([cot_own, cot_up1, cot_down1, cot_up2, cot_down2], 0, w_back, slope, None)
    cot_up3, cot_down3, mixed, out_far, *grads = tie(cot_up3, cot_down3, mixed, out_far, *grads)

    cot_far_up, cot_far_down = ring.up(cot_up3[:half]), ring.down(cot_down3[half:])
    moving = send(out_far)
    out_rest = out_part(rows, rest).astype(BF16)
    grads = back([cot_up3, cot_down3], pair(3), w_back, slope, grads)
    cot_far_up, cot_far_down, moving, out_rest, grads, mixed = tie(
        cot_far_up, cot_far_down, moving, out_rest, tuple(grads), mixed
    )

    moving = send(add(out_rest, 1, moving))
    d_attn, d_in, cot_all = back([cot_far_up, cot_far_down], row_of(far), w_back, slope, grads)
    d_in = attend_back(
        slots, reach, d_attn, query, keys, values, lse, start, cosine, sine, d_in, rows
    )
    moving, out_rest, d_in, cot_all, mixed = tie(moving, out_rest, d_in, cot_all, mixed)

    moving = send(add(out_rest, 2, moving))
    grad_far = split(grad_part(row_of(far), rows).astype(BF16))
    raw_in = tn_dot(normed_all, d_in).astype(BF16)
    moving, out_rest, grad_far, raw_in, d_in, cot_all, mixed = tie(
        moving, out_rest, grad_far, raw_in, d_in, cot_all, mixed
    )

    raw_in = lax.psum_scatter(raw_in, "dp", scatter_dimension=0, tiled=True)
    added = add(out_rest, 3, moving)
    *added, d_in = tie(*added, d_in)
    moving = send(added)
    grad_moving = send(grad_far)
    grad_rest = grad_part(rows, rest).astype(BF16)
    in_sum = jnp.sum(d_in, axis=0, dtype=F32)[None]
    moving, grad_moving, grad_rest, in_sum, mixed, cot_all, d_in = tie(
        moving, grad_moving, grad_rest, in_sum, mixed, cot_all, d_in
    )

    added = add(grad_rest, 1, grad_moving)
    *added, mixed, cot_all, moving, d_in, in_sum = tie(*added, mixed, cot_all, moving, d_in, in_sum)
    grad_moving = send(added)
    out_grad = tn_dot(mixed, cot_all).astype(BF16)
    summed = out_part(0, rows) + moving[0].astype(F32) + moving[1].astype(F32)
    output = (x_values + out_bias.astype(F32) + down_bias.astype(F32) + summed).astype(BF16)
    in_sum = exchange_sum(in_sum, "dp")
    grad_moving, in_sum, output, out_grad, d_in = tie(
        grad_moving, in_sum, output, out_grad, d_in
    )

    added = add(grad_rest, 2, grad_moving)
    out_grad = lax.psum_scatter(out_grad, "dp", scatter_dimension=1, tiled=True)
    *added, in_sum, d_in = tie(*added, in_sum, d_in)
    grad_moving = send(added)
    qkv_sum, up_sum = in_sum[:, :qkv_cols], in_sum[:, qkv_cols:]
    raw_qkv, raw_up = raw_in[:, :qkv_cols].astype(F32), raw_in[:, qkv_cols:].astype(F32)
    cot_values = cotangent.astype(F32)
    stats = jnp.stack(
        [
            jnp.sum(w_qkv * raw_qkv, axis=1),
            jnp.sum(w_qkv * qkv_sum, axis=1),
            jnp.sum(w_up * raw_up, axis=1),
            jnp.sum(w_up * up_sum, axis=1),
        ]
    )
    stats = exchange_rows(jnp.concatenate([stats, bias_part], axis=1), "dp")
    qkv_weight_grad = raw_qkv * gain1[:, None] + shift1[:, None] * qkv_sum
    bias_part = jnp.sum(stats[:, :, shard_rows:], axis=0).reshape(1, width)
    stats = jnp.transpose(stats[:, :, :shard_rows], (1, 0, 2)).reshape(4, width)
    stats = jnp.concatenate([stats, bias_part], axis=0)
    stats = stats + swap(stats, "tensor", 1)
    grad_last = grad_part(0, rows)
    grad_moving, stats, raw_in, grad_last = tie(grad_moving, stats, raw_in, grad_last)

    added = add(grad_rest, 3, grad_moving)
    *added, raw_in = tie(*added, raw_in)
    grad_moving = send(added)
    up_weight_grad = raw_up * gain2[:, None] + shift2[:, None] * up_sum
    stats, up_weight_grad = tie(stats, up_weight_grad)
    distances = range(2, ring.size, 2)
    stats = tree_sum([stats] + [swap(stats, "tensor", step) for step in distances])
    up_weight_grad, out_grad = tie(up_weight_grad, out_grad)
    out_grad = out_grad.astype(F32)
    out_weight_grad, down_weight_grad = out_grad[:HD], out_grad[HD:]
    grad_moving, stats, out_weight_grad, down_weight_grad = tie(
        grad_moving, stats, out_weight_grad, down_weight_grad
    )
    layer_input_gradient = finish(grad_last, *grad_moving, tokens, cotangent)
    return (
        output,
        layer_input_gradient,
        stats[0],
        stats[1],
        stats[2],
        stats[3],
        qkv_weight_grad.reshape(shard_rows, 1, qkv_cols),
        qkv_sum,
        out_weight_grad,
        stats[4],
        up_weight_grad,
        up_sum[0],
        down_weight_grad,
        stats[4],
    )


def solution(mesh):
    return jax.shard_map(
        body,
        mesh=mesh,
        in_specs=(
            P(("dp", "tensor"), None),
            P("dp", None),
            P(),
            P(),
            P(),
            P(),
            P("dp", "tensor", None),
            P("tensor", None),
            P("tensor", "dp"),
            P(),
            P("dp", "tensor"),
            P("tensor"),
            P("tensor", "dp"),
            P(),
            P(("dp", "tensor"), None),
        ),
        out_specs=(
            P(("dp", "tensor"), None),
            P(("dp", "tensor"), None),
            P(),
            P(),
            P(),
            P(),
            P("dp", "tensor", None),
            P("tensor", None),
            P("tensor", "dp"),
            P(),
            P("dp", "tensor"),
            P("tensor"),
            P("tensor", "dp"),
            P(),
        ),
        check_vma=False,
    )
```

```python
import functools
import math

import jax
import jax.numpy as jnp
from jax import lax
from jax.experimental import pallas as pl
from jax.experimental.pallas import tpu as pltpu
from jax.sharding import PartitionSpec as P

HD = 256
ROT = 64
LONGEST = 1024

NORM_EPS = 1e-05
MASK_FILL = -1e30
F32 = jnp.float32
BF16 = jnp.bfloat16
TILE = 256
MIB = 1024 * 1024
PROJECT_MIB = 36
BACK_MIB = 36
ATTEND_MIB = 20
ATTEND_BACK_MIB = 32


def normalize(values):
    mean_val = jnp.mean(values, axis=-1, keepdims=True)
    centred = values - mean_val
    spread = jnp.mean(centred * centred, axis=-1, keepdims=True)
    inv_std = lax.rsqrt(spread + NORM_EPS)
    return (centred * inv_std, inv_std)


def segment_starts(segment):
    row_count = segment.shape[0]
    position_index = jnp.arange(row_count, dtype=jnp.int32)
    starts = jnp.concatenate([jnp.ones((1,), dtype=jnp.bool_), segment[1:] != segment[:-1]])
    return lax.cummax(jnp.where(starts, position_index, jnp.zeros_like(position_index)), axis=0)


def rotation_tables(position):
    half_dims = ROT // 2
    lane = jnp.arange(128, dtype=jnp.int32)
    inv_freq = 10000.0 ** (-2.0 * (lane % half_dims).astype(F32) / ROT)
    angles = position.astype(F32)[:, None] * inv_freq[None, :]
    turned = (lane < ROT)[None, :]
    sign = jnp.where(lane < half_dims, -1.0, 1.0).astype(F32)[None, :]
    cosine = jnp.where(turned, jnp.cos(angles), 1.0)
    sine = jnp.where(turned, sign * jnp.sin(angles), 0.0)
    return cosine, sine


def turn(values, cosine, sine):
    head = values[:, :128]
    lane = lax.broadcasted_iota(jnp.int32, head.shape, 1)
    partner = jnp.where(
        lane < ROT // 2, pltpu.roll(head, 128 - ROT // 2, 1), pltpu.roll(head, ROT // 2, 1)
    )
    return jnp.concatenate([head * cosine + partner * sine, values[:, 128:]], axis=1)


def tie(*values):
    return lax.optimization_barrier(values)


def after(value, *others):
    return lax.optimization_barrier((value, others))[0]


def nt_dot(a, b):
    return lax.dot_general(a, b, (((1,), (1,)), ((), ())), preferred_element_type=F32)


def tn_dot(a, b):
    return lax.dot_general(a, b, (((0,), (0,)), ((), ())), preferred_element_type=F32)


def params(mib):
    return pltpu.CompilerParams(dimension_semantics=("arbitrary",), vmem_limit_bytes=mib * MIB)


def in_hbm(*values):
    return [pltpu.with_memory_space_constraint(value, pltpu.HBM) for value in values]


def fill(ins, rows_ref):
    at = 0
    for ref in ins:
        rows_ref[at : at + ref.shape[0], :] = ref[...]
        at += ref.shape[0]


def project_kernel(pieces, qkv_tiles, refs):
    w_ref, bias_ref = refs[pieces], refs[pieces + 1]
    proj_ref, mixed_ref, slope_ref, rows_ref = refs[-4:]
    j = pl.program_id(0)

    @pl.when(j == 0)
    def _():
        fill(refs[:pieces], rows_ref)

    def product():
        return jnp.dot(rows_ref[...], w_ref[...], preferred_element_type=F32) + bias_ref[...]

    @pl.when(j < qkv_tiles)
    def _():
        proj_ref[...] = product()

    @pl.when(j >= qkv_tiles)
    def _():
        out = product()
        cdf = 0.5 * (1.0 + lax.erf(out * (1.0 / math.sqrt(2.0))))
        mixed_ref[...] = (out * cdf).astype(BF16)
        density = jnp.exp(-0.5 * out * out) * (1.0 / math.sqrt(2.0 * math.pi))
        slope_ref[...] = (cdf + out * density).astype(BF16)


def aligned(col):
    return pl.multiple_of(col, TILE)


def at_element(rows, cols, index):
    return pl.BlockSpec((pl.Element(rows), pl.Element(cols)), index)


def in_place(kernel, grid, pieces, row, extra, extra_specs, bufs, buf_types, out_specs, mib, cost, name):
    given = () if bufs is None else tuple(bufs)
    first = len(pieces) + len(extra)
    return pl.pallas_call(
        lambda *refs: kernel(refs),
        grid=grid,
        in_specs=[pl.BlockSpec(piece.shape, lambda j: (0, 0)) for piece in pieces]
        + extra_specs
        + [pl.BlockSpec(memory_space=pltpu.HBM)] * len(given),
        out_specs=out_specs,
        out_shape=[pltpu.HBM(shape, dtype) for shape, dtype in buf_types],
        input_output_aliases={first + i: i for i in range(len(given))},
        compiler_params=params(mib),
        cost_estimate=cost,
        name=name,
    )(*in_hbm(*pieces, *extra), *given)


def project(pieces, row, weight, bias, group_rows, bufs):
    width, cols = weight.shape
    count = sum(piece.shape[0] for piece in pieces)
    qkv_tiles = 3 * HD // TILE
    hidden = cols - 3 * HD
    up_tile = lambda j: jnp.maximum(j - qkv_tiles, 0) * TILE
    return in_place(
        functools.partial(project_kernel, len(pieces), qkv_tiles),
        (cols // TILE,),
        pieces,
        row,
        (weight, bias),
        [
            pl.BlockSpec((width, TILE), lambda j: (0, j)),
            pl.BlockSpec((1, TILE), lambda j: (0, j)),
        ],
        bufs,
        [
            ((group_rows, 3 * HD), F32),
            ((group_rows, HD + hidden), BF16),
            ((group_rows, hidden), BF16),
            ((group_rows, width), BF16),
        ],
        [
            at_element(count, TILE, lambda j: (row, aligned(jnp.minimum(j, qkv_tiles - 1) * TILE))),
            at_element(count, TILE, lambda j: (row, aligned(HD + up_tile(j)))),
            at_element(count, TILE, lambda j: (row, aligned(up_tile(j)))),
            at_element(count, width, lambda j: (row, 0)),
        ],
        PROJECT_MIB,
        pl.CostEstimate(
            flops=2 * count * width * cols,
            bytes_accessed=2 * (width * cols + 2 * count * width) + 8 * count * cols // 2,
            transcendentals=2 * count * hidden,
        ),
        "project",
    )


def back_kernel(pieces, refs):
    w_ref, slope_ref = refs[pieces], refs[pieces + 1]
    attn_ref, d_in_ref, rows_ref = refs[-3:]
    j = pl.program_id(0)

    @pl.when(j == 0)
    def _():
        fill(refs[:pieces], rows_ref)

    out = jnp.dot(rows_ref[...], w_ref[...], preferred_element_type=F32)

    @pl.when(j == 0)
    def _():
        attn_ref[...] = out.astype(BF16)

    @pl.when(j > 0)
    def _():
        d_in_ref[...] = (out * slope_ref[...].astype(F32)).astype(BF16)


def back(pieces, row, weight, slope, bufs):
    width, cols = weight.shape
    group_rows, hidden = slope.shape
    count = sum(piece.shape[0] for piece in pieces)
    up_tile = lambda j: jnp.maximum(j - 1, 0) * TILE
    return in_place(
        functools.partial(back_kernel, len(pieces)),
        (cols // TILE,),
        pieces,
        row,
        (weight, slope),
        [
            pl.BlockSpec((width, TILE), lambda j: (0, j)),
            at_element(count, TILE, lambda j: (row, aligned(up_tile(j)))),
        ],
        bufs,
        [
            ((group_rows, HD), BF16),
            ((group_rows, 3 * HD + hidden), BF16),
            ((group_rows, width), BF16),
        ],
        [
            at_element(count, HD, lambda j: (row, 0)),
            at_element(count, TILE, lambda j: (row, aligned(3 * HD + up_tile(j)))),
            at_element(count, width, lambda j: (row, 0)),
        ],
        BACK_MIB,
        pl.CostEstimate(
            flops=2 * count * width * cols,
            bytes_accessed=2 * (width * cols + 2 * count * width + 3 * count * cols),
            transcendentals=0,
        ),
        "back",
    )


def window_mask(block, rows, count, start_ref):
    shape = (rows, count * rows)
    key_at = (block - count + 1) * rows + lax.broadcasted_iota(jnp.int32, shape, 1)
    query_at = block * rows + lax.broadcasted_iota(jnp.int32, shape, 0)
    return (key_at >= start_ref[:, :1]) & (key_at <= query_at)


def by_count(reach_ref, rows, visit):
    block = pl.program_id(0)
    for count in range(1, LONGEST // rows + 2):

        @pl.when(reach_ref[block] == count)
        def _():
            first = pl.multiple_of((block - count + 1) * rows, rows)
            visit(count, pl.ds(first, count * rows))


def attend_kernel(
    rows, slot_ref, reach_ref, proj_ref, cos_ref, sin_ref, start_ref, _,
    mixed_ref, q_ref, k_ref, v_ref, lse_ref,
):
    block = pl.program_id(0)
    cosine, sine = cos_ref[...], sin_ref[...]
    here = pl.ds(pl.multiple_of(block * rows, rows), rows)
    q_ref[...] = turn(proj_ref[:, :HD], cosine, sine).astype(BF16)
    k_ref[here, :] = turn(proj_ref[:, HD : 2 * HD], cosine, sine).astype(BF16)
    v_ref[here, :] = proj_ref[:, 2 * HD :].astype(BF16)

    def visit(count, window):
        scores = nt_dot(q_ref[...], k_ref[window, :]) * (1.0 / math.sqrt(HD))
        scores = jnp.where(window_mask(block, rows, count, start_ref), scores, MASK_FILL)
        top = jnp.max(scores, axis=1, keepdims=True)
        weights = jnp.exp(scores - top)
        total = jnp.sum(weights, axis=1, keepdims=True)
        low = (weights * (1.0 / total)).astype(BF16)
        mixed_ref[...] = jnp.dot(low, v_ref[window, :], preferred_element_type=F32).astype(BF16)
        lse_ref[...] = top + jnp.log(total)

    by_count(reach_ref, rows, visit)


def attend(slots, reach, proj, cosine, sine, start, mixed, rows):
    group_rows = proj.shape[0]
    by_slot = lambda i, slot, reach: (slot[i], 0)
    in_order = lambda i, slot, reach: (i, 0)
    whole = lambda i, slot, reach: (0, 0)
    return pl.pallas_call(
        functools.partial(attend_kernel, rows),
        grid_spec=pltpu.PrefetchScalarGridSpec(
            num_scalar_prefetch=2,
            grid=(group_rows // rows,),
            in_specs=[
                pl.BlockSpec((rows, 3 * HD), by_slot),
                pl.BlockSpec((rows, 128), in_order),
                pl.BlockSpec((rows, 128), in_order),
                pl.BlockSpec((rows, 128), in_order),
                pl.BlockSpec(memory_space=pltpu.HBM),
            ],
            out_specs=[
                pl.BlockSpec((rows, HD), by_slot),
                pl.BlockSpec((rows, HD), in_order),
                pl.BlockSpec((group_rows, HD), whole),
                pl.BlockSpec((group_rows, HD), whole),
                pl.BlockSpec((rows, 1), in_order),
            ],
        ),
        out_shape=[
            pltpu.HBM(mixed.shape, BF16),
            pltpu.HBM((group_rows, HD), BF16),
            pltpu.HBM((group_rows, HD), BF16),
            pltpu.HBM((group_rows, HD), BF16),
            pltpu.HBM((group_rows, 1), F32),
        ],
        input_output_aliases={6: 0},
        compiler_params=params(ATTEND_MIB),
        cost_estimate=pl.CostEstimate(
            flops=4 * group_rows * LONGEST * HD,
            bytes_accessed=group_rows * HD * 22,
            transcendentals=group_rows * LONGEST,
        ),
        name="attend",
    )(slots, reach, *in_hbm(proj, cosine, sine, start), mixed)


def attend_back_kernel(
    rows, slot_ref, reach_ref, d_attn_ref, q_ref, k_ref, v_ref, lse_ref, start_ref, cos_ref, sin_ref,
    _, d_proj_ref, dk_ref, dv_ref,
):
    block = pl.program_id(0)
    blocks = pl.num_programs(0)
    scale = 1.0 / math.sqrt(HD)
    here = pl.ds(pl.multiple_of(block * rows, rows), rows)
    slot = pl.ds(pl.multiple_of(slot_ref[block] * rows, rows), rows)
    dk_ref[here, :] = jnp.zeros((rows, HD), F32)
    dv_ref[here, :] = jnp.zeros((rows, HD), F32)

    def visit(count, window):
        query, d_attn, keys = q_ref[...], d_attn_ref[...], k_ref[window, :]
        scores = nt_dot(query, keys) * scale
        mask = window_mask(block, rows, count, start_ref)
        probs = jnp.exp(jnp.where(mask, scores - lse_ref[...], MASK_FILL))
        d_probs = nt_dot(d_attn, v_ref[window, :])
        inner = jnp.sum(probs * d_probs, axis=1, keepdims=True)
        d_scores = (probs * (d_probs - inner)).astype(BF16)
        d_query = jnp.dot(d_scores, keys, preferred_element_type=F32) * scale
        dk_ref[window, :] += tn_dot(d_scores, query)
        dv_ref[window, :] += tn_dot(probs.astype(BF16), d_attn)
        d_proj_ref[slot, :HD] = turn(d_query, cos_ref[here, :], -sin_ref[here, :]).astype(BF16)

    by_count(reach_ref, rows, visit)

    @pl.when(block == blocks - 1)
    def _():
        def finish(i, carry):
            own = pl.ds(pl.multiple_of(i * rows, rows), rows)
            to = pl.ds(pl.multiple_of(slot_ref[i] * rows, rows), rows)
            d_key = turn(dk_ref[own, :] * scale, cos_ref[own, :], -sin_ref[own, :])
            d_proj_ref[to, HD : 2 * HD] = d_key.astype(BF16)
            d_proj_ref[to, 2 * HD :] = dv_ref[own, :].astype(BF16)
            return carry

        lax.fori_loop(0, blocks, finish, 0)


def attend_back(slots, reach, d_attn, query, keys, values, lse, start, cosine, sine, d_in, rows):
    group_rows = query.shape[0]
    by_slot = lambda i, slot, reach: (slot[i], 0)
    in_order = lambda i, slot, reach: (i, 0)
    whole = lambda i, slot, reach: (0, 0)
    return pl.pallas_call(
        functools.partial(attend_back_kernel, rows),
        grid_spec=pltpu.PrefetchScalarGridSpec(
            num_scalar_prefetch=2,
            grid=(group_rows // rows,),
            in_specs=[
                pl.BlockSpec((rows, HD), by_slot),
                pl.BlockSpec((rows, HD), in_order),
                pl.BlockSpec((group_rows, HD), whole),
                pl.BlockSpec((group_rows, HD), whole),
                pl.BlockSpec((rows, 1), in_order),
                pl.BlockSpec((rows, 128), in_order),
                pl.BlockSpec((group_rows, 128), whole),
                pl.BlockSpec((group_rows, 128), whole),
                pl.BlockSpec(memory_space=pltpu.HBM),
            ],
            out_specs=pl.BlockSpec((group_rows, 3 * HD), whole),
            scratch_shapes=[pltpu.VMEM((group_rows, HD), F32), pltpu.VMEM((group_rows, HD), F32)],
        ),
        out_shape=pltpu.HBM(d_in.shape, BF16),
        input_output_aliases={10: 0},
        compiler_params=params(ATTEND_BACK_MIB),
        cost_estimate=pl.CostEstimate(
            flops=10 * group_rows * LONGEST * HD,
            bytes_accessed=group_rows * HD * 20,
            transcendentals=group_rows * LONGEST,
        ),
        name="attend_back",
    )(slots, reach, *in_hbm(d_attn, query, keys, values, lse, start, cosine, sine), d_in)


def finish_kernel(own_ref, up_ref, down_ref, tokens_ref, cot_ref, out_ref):
    normed, inv_std = normalize(tokens_ref[...].astype(F32))
    total = own_ref[...] + up_ref[...].astype(F32) + down_ref[...].astype(F32)
    out_ref[...] = cot_ref[...].astype(F32) + inv_std * (
        total
        - jnp.mean(total, axis=1, keepdims=True)
        - normed * jnp.mean(total * normed, axis=1, keepdims=True)
    )


def finish(own, up, down, tokens, cotangent):
    rows, width = tokens.shape
    step = rows // 2
    spec = pl.BlockSpec((step, width), lambda i: (i, 0))
    return pl.pallas_call(
        finish_kernel,
        grid=(rows // step,),
        in_specs=[spec] * 5,
        out_specs=spec,
        out_shape=jax.ShapeDtypeStruct((rows, width), F32),
        compiler_params=params(20),
        cost_estimate=pl.CostEstimate(
            flops=16 * rows * width, bytes_accessed=16 * rows * width, transcendentals=rows
        ),
        name="finish",
    )(own, up, down, tokens, cotangent)


class Ring:
    def __init__(self, axis):
        self.axis = axis
        size = lax.axis_size(axis)
        order = list(range(0, size, 2)) + list(range(size - 1, 0, -2))
        place = [order.index(i) for i in range(size)]
        self.size, self.far = size, size // 2
        self.up_pairs = [(order[i], order[(i + 1) % size]) for i in range(size)]
        self.down_pairs = [(order[i], order[(i - 1) % size]) for i in range(size)]
        slot_of = [0] * size
        for offset in range(size):
            slot_of[offset] = self.slot(offset)
        here = jnp.array(place, jnp.int32)[lax.axis_index(axis)]
        offsets = (jnp.array(place, jnp.int32) - here + size) % size
        self.slots = jnp.array(slot_of, jnp.int32)[offsets]

    def slot(self, offset):
        offset %= self.size
        if offset == 0:
            return 0
        if offset == self.far:
            return self.size - 1
        return 2 * offset if offset < self.far else 2 * (self.size - offset) - 1

    def up(self, value):
        return lax.ppermute(value, self.axis, self.up_pairs)

    def down(self, value):
        return lax.ppermute(value, self.axis, self.down_pairs)


def swap(value, axis, step):
    return lax.ppermute(value, axis, [(i, i ^ step) for i in range(lax.axis_size(axis))])


def from_all(value, axis):
    return [value] + [swap(value, axis, step) for step in range(1, lax.axis_size(axis))]


def tree_sum(values):
    while len(values) > 1:
        values = [a + b for a, b in zip(values[0::2], values[1::2])]
    return values[0]


def exchange_sum(value, axis):
    return tree_sum(from_all(value, axis))


def exchange_rows(value, axis):
    values = from_all(value, axis)
    me = lax.axis_index(axis)
    whole = jnp.zeros((len(values),) + value.shape, value.dtype)
    for distance, piece in enumerate(values):
        whole = lax.dynamic_update_index_in_dim(whole, piece, me ^ distance, 0)
    return whole


def body(
    tokens,
    segment_ids,
    first_gain,
    first_shift,
    second_gain,
    second_shift,
    qkv_weight,
    qkv_bias,
    out_weight,
    out_bias,
    up_projection_weight,
    up_bias,
    down_weight,
    down_bias,
    cotangent,
):
    rows, width = tokens.shape
    qkv_cols = 3 * HD
    segment = segment_ids[0]
    group_rows = segment.shape[0]
    ring = Ring("tensor")
    far = ring.far
    half = rows // 2
    shard_rows = qkv_weight.shape[0]
    dp_start = lax.axis_index("dp") * shard_rows

    x_values = tokens.astype(F32)
    normed, inv_std = normalize(x_values)
    normed_low = normed.astype(BF16)
    up1, down1 = ring.up(normed_low), ring.down(normed_low)

    w_qkv = qkv_weight.reshape(shard_rows, qkv_cols).astype(F32)
    w_up = up_projection_weight.astype(F32)

    def shard(vector):
        return lax.dynamic_slice(vector, (dp_start,), (shard_rows,)).astype(F32)

    gain1, gain2 = shard(first_gain), shard(second_gain)
    shift1, shift2 = shard(first_shift), shard(second_shift)
    scaled = jnp.concatenate(
        [w_qkv * gain1[:, None], w_up * gain2[:, None]], axis=1
    ).astype(BF16)
    w_in = lax.all_gather(scaled, "dp", axis=0, tiled=True)
    def row_of(offset):
        return ring.slot(offset) * rows

    def pair(step):
        return row_of(-step)

    w_out = after(jnp.concatenate([out_weight.T, down_weight.T], axis=1), scaled)
    shift_part = jnp.concatenate(
        [jnp.sum(w_qkv * shift1[:, None], axis=0), jnp.sum(w_up * shift2[:, None], axis=0)]
    )
    up1, down1, w_out, shift_part, slots = tie(up1, down1, w_out, shift_part, ring.slots)
    up2, down2 = ring.up(up1), ring.down(down1)
    w_back = lax.all_gather(w_out, "dp", axis=0, tiled=True)
    start = segment_starts(after(segment, up1))
    cosine, sine = rotation_tables(jnp.arange(group_rows, dtype=jnp.int32) - start)
    cosine, sine, shift_part = tie(cosine, sine, shift_part)
    in_bias = exchange_sum(shift_part[None], "dp") + jnp.concatenate(
        [qkv_bias.reshape(-1), up_bias]
    ).astype(F32)[None]
    block_at = jnp.arange(group_rows // rows, dtype=jnp.int32)
    reach = jnp.clip(block_at - start[::rows] // rows + 1, 1, LONGEST // rows + 1)
    start = jnp.broadcast_to(start[:, None], cosine.shape)
    up2, down2, cosine, sine, start, in_bias, slots, reach = tie(
        up2, down2, cosine, sine, start, in_bias, slots, reach
    )

    up3, down3 = ring.up(up2), ring.down(down2)
    bufs = project([after(normed_low, up2), up1, down1], 0, w_in, in_bias, group_rows, None)
    up3, down3, *bufs = tie(up3, down3, *bufs)

    far_up, far_down = ring.up(up3[:half]), ring.down(down3[half:])
    cot_own = after(cotangent, up3, down3)
    cot_up1, cot_down1 = ring.up(cot_own), ring.down(cot_own)
    bufs = project([up2, down2, up3, down3], pair(2), w_in, in_bias, group_rows, bufs)
    bias_part = jnp.sum(cot_own, axis=0, dtype=F32).reshape(4, -1)
    far_up, far_down, cot_up1, cot_down1, bias_part, *bufs = tie(
        far_up, far_down, cot_up1, cot_down1, bias_part, *bufs
    )

    cot_up2, cot_down2 = ring.up(cot_up1), ring.down(cot_down1)
    bufs = project([far_up, far_down], row_of(far), w_in, in_bias, group_rows, bufs)
    proj, mixed, slope, normed_all = bufs
    mixed, query, keys, values, lse = attend(slots, reach, proj, cosine, sine, start, mixed, rows)
    cot_up2, cot_down2, mixed, slope = tie(cot_up2, cot_down2, mixed, slope)

    def split(block):
        return block[:half], block[half:]

    def send(pair_of_rows):
        return ring.up(pair_of_rows[0]), ring.down(pair_of_rows[1])

    def add(parts, step, moving):
        moving = [value.astype(F32) for value in moving]
        if step == 1:
            moving = [
                jnp.pad(moving[0], ((0, rows - half), (0, 0))),
                jnp.pad(moving[1], ((half, 0), (0, 0))),
            ]
        at = [row_of(far - step), row_of(step - far)]
        return tuple(
            (parts[first - rows : first].astype(F32) + value).astype(BF16)
            for first, value in zip(at, moving)
        )

    def out_part(first, count):
        return nt_dot(mixed[first : first + count], w_back)

    def grad_part(first, count):
        return nt_dot(d_in[first : first + count], w_in)

    rest = group_rows - 2 * rows

    cot_up3, cot_down3 = ring.up(cot_up2), ring.down(cot_down2)
    out_far = split(out_part(row_of(far), rows).astype(BF16))
    grads = back([cot_own, cot_up1, cot_down1, cot_up2, cot_down2], 0, w_back, slope, None)
    cot_up3, cot_down3, mixed, out_far, *grads = tie(cot_up3, cot_down3, mixed, out_far, *grads)

    cot_far_up, cot_far_down = ring.up(cot_up3[:half]), ring.down(cot_down3[half:])
    moving = send(out_far)
    out_rest = out_part(rows, rest).astype(BF16)
    grads = back([cot_up3, cot_down3], pair(3), w_back, slope, grads)
    cot_far_up, cot_far_down, moving, out_rest, grads, mixed = tie(
        cot_far_up, cot_far_down, moving, out_rest, tuple(grads), mixed
    )

    moving = send(add(out_rest, 1, moving))
    d_attn, d_in, cot_all = back([cot_far_up, cot_far_down], row_of(far), w_back, slope, grads)
    d_in = attend_back(
        slots, reach, d_attn, query, keys, values, lse, start, cosine, sine, d_in, rows
    )
    moving, out_rest, d_in, cot_all, mixed = tie(moving, out_rest, d_in, cot_all, mixed)

    moving = send(add(out_rest, 2, moving))
    grad_far = split(grad_part(row_of(far), rows).astype(BF16))
    raw_in = tn_dot(normed_all, d_in).astype(BF16)
    moving, out_rest, grad_far, raw_in, d_in, cot_all, mixed = tie(
        moving, out_rest, grad_far, raw_in, d_in, cot_all, mixed
    )

    raw_in = lax.psum_scatter(raw_in, "dp", scatter_dimension=0, tiled=True)
    added = add(out_rest, 3, moving)
    *added, d_in = tie(*added, d_in)
    moving = send(added)
    grad_moving = send(grad_far)
    grad_rest = grad_part(rows, rest).astype(BF16)
    in_sum = jnp.sum(d_in, axis=0, dtype=F32)[None]
    moving, grad_moving, grad_rest, in_sum, mixed, cot_all, d_in = tie(
        moving, grad_moving, grad_rest, in_sum, mixed, cot_all, d_in
    )

    added = add(grad_rest, 1, grad_moving)
    *added, mixed, cot_all, moving, d_in, in_sum = tie(*added, mixed, cot_all, moving, d_in, in_sum)
    grad_moving = send(added)
    out_grad = tn_dot(mixed, cot_all).astype(BF16)
    summed = out_part(0, rows) + moving[0].astype(F32) + moving[1].astype(F32)
    output = (x_values + out_bias.astype(F32) + down_bias.astype(F32) + summed).astype(BF16)
    in_sum = exchange_sum(in_sum, "dp")
    grad_moving, in_sum, output, out_grad, d_in = tie(
        grad_moving, in_sum, output, out_grad, d_in
    )

    added = add(grad_rest, 2, grad_moving)
    out_grad = lax.psum_scatter(out_grad, "dp", scatter_dimension=1, tiled=True)
    *added, in_sum, d_in = tie(*added, in_sum, d_in)
    grad_moving = send(added)
    qkv_sum, up_sum = in_sum[:, :qkv_cols], in_sum[:, qkv_cols:]
    raw_qkv, raw_up = raw_in[:, :qkv_cols].astype(F32), raw_in[:, qkv_cols:].astype(F32)
    cot_values = cotangent.astype(F32)
    stats = jnp.stack(
        [
            jnp.sum(w_qkv * raw_qkv, axis=1),
            jnp.sum(w_qkv * qkv_sum, axis=1),
            jnp.sum(w_up * raw_up, axis=1),
            jnp.sum(w_up * up_sum, axis=1),
        ]
    )
    stats = exchange_rows(jnp.concatenate([stats, bias_part], axis=1), "dp")
    qkv_weight_grad = raw_qkv * gain1[:, None] + shift1[:, None] * qkv_sum
    bias_part = jnp.sum(stats[:, :, shard_rows:], axis=0).reshape(1, width)
    stats = jnp.transpose(stats[:, :, :shard_rows], (1, 0, 2)).reshape(4, width)
    stats = jnp.concatenate([stats, bias_part], axis=0)
    stats = stats + swap(stats, "tensor", 1)
    grad_last = grad_part(0, rows)
    grad_moving, stats, raw_in, grad_last = tie(grad_moving, stats, raw_in, grad_last)

    added = add(grad_rest, 3, grad_moving)
    *added, raw_in = tie(*added, raw_in)
    grad_moving = send(added)
    up_weight_grad = raw_up * gain2[:, None] + shift2[:, None] * up_sum
    stats, up_weight_grad = tie(stats, up_weight_grad)
    distances = range(2, ring.size, 2)
    stats = tree_sum([stats] + [swap(stats, "tensor", step) for step in distances])
    up_weight_grad, out_grad = tie(up_weight_grad, out_grad)
    out_grad = out_grad.astype(F32)
    out_weight_grad, down_weight_grad = out_grad[:HD], out_grad[HD:]
    grad_moving, stats, out_weight_grad, down_weight_grad = tie(
        grad_moving, stats, out_weight_grad, down_weight_grad
    )
    layer_input_gradient = finish(grad_last, *grad_moving, tokens, cotangent)
    return (
        output,
        layer_input_gradient,
        stats[0],
        stats[1],
        stats[2],
        stats[3],
        qkv_weight_grad.reshape(shard_rows, 1, qkv_cols),
        qkv_sum,
        out_weight_grad,
        stats[4],
        up_weight_grad,
        up_sum[0],
        down_weight_grad,
        stats[4],
    )


def solution(mesh):
    return jax.shard_map(
        body,
        mesh=mesh,
        in_specs=(
            P(("dp", "tensor"), None),
            P("dp", None),
            P(),
            P(),
            P(),
            P(),
            P("dp", "tensor", None),
            P("tensor", None),
            P("tensor", "dp"),
            P(),
            P("dp", "tensor"),
            P("tensor"),
            P("tensor", "dp"),
            P(),
            P(("dp", "tensor"), None),
        ),
        out_specs=(
            P(("dp", "tensor"), None),
            P(("dp", "tensor"), None),
            P(),
            P(),
            P(),
            P(),
            P("dp", "tensor", None),
            P("tensor", None),
            P("tensor", "dp"),
            P(),
            P("dp", "tensor"),
            P("tensor"),
            P("tensor", "dp"),
            P(),
        ),
        check_vma=False,
    )
```
